512 devices in a mesh: tm: 16 (over x, y_lo, core), slab: 32 (over z, y_hi).
Axes of the slice: x: 4, y: 4 (y_hi: 2, y_lo: 2; y = y_hi * 2 + y_lo), z: 16, core: 2. Of those that a mesh axis runs over, the one named last changes fastest.
Arguments:
- node_values: float32 [16, 3, 2, 128, 16, 128], P('tm', None, None, 'slab'), may hold values from 0 to 1
- start_state: float32 [16, 2, 128, 16, 128], P('tm', None, 'slab'), may hold values from 0 to 1
- feed_rate: float32 [128, 16, 128], P('slab'), may hold values from 0.02 to 0.08
- kill_rate: float32 [128, 16, 128], P('slab'), may hold values from 0.03 to 0.1
Outputs:
- swept_nodes: float32 [16, 3, 2, 128, 16, 128], P('tm', None, None, 'slab')
The draws below stay inside these ranges and needn't reach their ends.
All inputs are finite; a program needn't handle non-finite values.
Results may differ from the reference program's by a relative error of at most 0.0003.
Values sent between devices are 32-bit elements; how exact they have to be, the bound alone decides.
No kernel may reach another device: no remote copies, remote signals or barrier semaphores. Data moves between devices by JAX's collectives and lax.ppermute only.
A program may use at most 64 MiB of HBM per device.

```python
import math
import jax
import jax.numpy as jnp
from jax import lax

CX = 16
CY = 128
SOLVES = 2
NZ = 128
SLICES = 16


def block_levels(rng, shape, cuts, least, high):
    factor_of = 1.0
    for dim, parts in cuts:
        steps = jax.random.uniform(jax.random.fold_in(jax.random.fold_in(rng, 6), dim), (parts,), jnp.float32, least / len(cuts), high / len(cuts))
        factor_of = factor_of * jnp.repeat(jnp.exp(steps), shape[dim] // parts).reshape((-1,) + (1,) * (len(shape) - 1 - dim))
    return factor_of


def setup_inputs(seed: int = 0) -> dict:
    streams_of = jax.random.split(jax.random.key(seed), 5)
    return {
        "node_values": jnp.clip(1.0 * jax.random.uniform(streams_of[0], (SLICES, 3, 2, NZ, CX, CY), jnp.float32) ** block_levels(streams_of[0], (SLICES, 3, 2, NZ, CX, CY), ((0, 16), (3, 32)), -0.2, 0.2), 0.0, 1.0),
        "start_state": jnp.clip(1.0 * jax.random.uniform(streams_of[1], (SLICES, 2, NZ, CX, CY), jnp.float32) ** block_levels(streams_of[1], (SLICES, 2, NZ, CX, CY), ((0, 16), (2, 32)), -0.2, 0.2), 0.0, 1.0),
        "feed_rate": jnp.clip(jnp.exp(math.log(0.08) - 1.3862944 * jax.random.uniform(streams_of[2], (NZ, CX, CY), jnp.float32) ** block_levels(streams_of[2], (NZ, CX, CY), ((0, 32),), -0.2, 0.2)), 0.02, 0.08),
        "kill_rate": jnp.clip(jnp.exp(math.log(0.1) - 1.2039728 * jax.random.uniform(streams_of[3], (NZ, CX, CY), jnp.float32) ** block_levels(streams_of[3], (NZ, CX, CY), ((0, 32),), -0.2, 0.2)), 0.03, 0.1),
    }


slice_length = 2.0
half_step = 1.0
weights_first = (5.0 / 24.0, 1.0 / 3.0, -1.0 / 24.0)
weights_second = (-1.0 / 24.0, 1.0 / 3.0, 5.0 / 24.0)
diffusion = (0.1, 0.05)


def stencil_line(values, dimension):
    nearest = jnp.roll(values, 1, axis=dimension) + jnp.roll(values, -1, axis=dimension)
    farther = jnp.roll(values, 2, axis=dimension) + jnp.roll(values, -2, axis=dimension)
    return (16.0 * nearest - farther - 30.0 * values) / 12.0


def stencil_depth(padded):
    middle = padded[..., 2:-2, :, :]
    nearest = padded[..., 1:-3, :, :] + padded[..., 3:-1, :, :]
    farther = padded[..., :-4, :, :] + padded[..., 4:, :, :]
    return (16.0 * nearest - farther - 30.0 * middle) / 12.0


def explicit_term(padded, spread):
    middle = padded[..., 2:-2, :, :]
    laplace = spread * (stencil_depth(padded) + stencil_line(middle, -2)) + stencil_line(middle, -1)
    coefficient = jnp.array(diffusion, dtype=jnp.float32).reshape(2, 1, 1, 1)
    return coefficient * laplace


def reaction(fields, feed_rate, kill_rate):
    substrate = fields[..., 0, :, :, :]
    catalyst = fields[..., 1, :, :, :]
    growth = substrate * catalyst * catalyst
    return jnp.stack([feed_rate * (1.0 - substrate) - growth, growth - (feed_rate + kill_rate) * catalyst], axis=-4)


def node_solve(target, initial, feed_rate, kill_rate):
    substrate = initial[0]
    catalyst = initial[1]
    for repeat_index in range(SOLVES):
        growth = substrate * catalyst * catalyst
        substrate_next = (target[0] + half_step * (feed_rate - growth)) / (1.0 + half_step * feed_rate)
        catalyst_next = (target[1] + half_step * growth) / (1.0 + half_step * (feed_rate + kill_rate))
        substrate, catalyst = substrate_next, catalyst_next
    return jnp.stack([substrate, catalyst])


def restrict(values):
    extent = values.shape
    blocks = values.reshape(extent[:-3] + (extent[-3] // 2, 2, extent[-2] // 2, 2, extent[-1]))
    return 0.25 * (blocks[..., 0, :, 0, :] + blocks[..., 0, :, 1, :] + blocks[..., 1, :, 0, :] + blocks[..., 1, :, 1, :])


def prolong(values):
    extent = values.shape
    widened = jnp.broadcast_to(values[..., :, None, :, None, :], extent[:-3] + (extent[-3], 2, extent[-2], 2, extent[-1]))
    return widened.reshape(extent[:-3] + (2 * extent[-3], 2 * extent[-2], extent[-1]))


def weighted(weights, tendency):
    return slice_length * (weights[0] * tendency[0] + weights[1] * tendency[1] + weights[2] * tendency[2])


def wrap_depth(values):
    return jnp.concatenate([values[..., -2:, :, :], values, values[..., :2, :, :]], axis=-3)


def tendency_of(fields, feed_rate, kill_rate, spread):
    return explicit_term(wrap_depth(fields), spread) + reaction(fields, feed_rate, kill_rate)


def sweep(previous, start, feed_rate, kill_rate, spread, fas_term):
    explicit_old = explicit_term(wrap_depth(previous), spread)
    tendency = explicit_old + reaction(previous, feed_rate, kill_rate)
    integral_one = weighted(weights_first, tendency) + fas_term[0]
    integral_two = weighted(weights_second, tendency) + fas_term[1]
    explicit_start = explicit_term(wrap_depth(start[None]), spread)[0]
    target = start + half_step * (explicit_start - explicit_old[0]) - half_step * reaction(previous[1], feed_rate, kill_rate) + integral_one
    first_node = node_solve(target, previous[1], feed_rate, kill_rate)
    explicit_first = explicit_term(wrap_depth(first_node[None]), spread)[0]
    target = first_node + half_step * (explicit_first - explicit_old[1]) - half_step * reaction(previous[2], feed_rate, kill_rate) + integral_two
    second_node = node_solve(target, previous[2], feed_rate, kill_rate)
    return jnp.stack([start, first_node, second_node])


def reference(node_values, start_state, feed_rate, kill_rate):
    coarse_feed = restrict(feed_rate)
    coarse_kill = restrict(kill_rate)
    fine_zero = jnp.zeros((2,) + start_state.shape[1:], jnp.float32)

    def first_phase(inputs):
        previous, start = inputs
        swept = sweep(previous, start, feed_rate, kill_rate, 1.0, fine_zero)
        fine_tendency = tendency_of(swept, feed_rate, kill_rate, 1.0)
        coarse_old = restrict(swept)
        coarse_tendency = tendency_of(coarse_old, coarse_feed, coarse_kill, 0.25)
        fas_term = jnp.stack([
            restrict(weighted(weights_first, fine_tendency)) - weighted(weights_first, coarse_tendency),
            restrict(weighted(weights_second, fine_tendency)) - weighted(weights_second, coarse_tendency)])
        return swept, coarse_old, fas_term

    swept_all, coarse_all, fas_all = lax.map(first_phase, (node_values, start_state))

    def chain_turn(begin_state, inputs):
        coarse_old, fas_term = inputs
        updated = sweep(coarse_old, begin_state, coarse_feed, coarse_kill, 0.25, fas_term)
        return updated[2], updated

    last_state, coarse_new = lax.scan(chain_turn, restrict(start_state[0]), (coarse_all, fas_all))
    end_states = swept_all[:, 2] + prolong(coarse_new[:, 2] - coarse_all[:, 2])
    starts = jnp.concatenate([start_state[:1], end_states[:-1]], axis=0)

    def second_phase(inputs):
        swept, coarse_old, coarse_updated, start = inputs
        previous = swept + prolong(coarse_updated - coarse_old)
        return sweep(previous, start, feed_rate, kill_rate, 1.0, fine_zero)

    return lax.map(second_phase, (swept_all, coarse_all, coarse_new, starts))
```

```python
import jax
import jax.numpy as jnp
from jax import lax
from jax.experimental import pallas as pl
from jax.experimental.pallas import tpu as pltpu
from jax.sharding import PartitionSpec as P

AX = ("tm", "slab")
F32 = jnp.float32
W1 = (5.0 / 12.0, 2.0 / 3.0, -1.0 / 12.0)
W2 = (-1.0 / 12.0, 2.0 / 3.0, 5.0 / 12.0)
R1 = (5.0 / 12.0, 2.0 / 3.0 - 1.0, -1.0 / 12.0)
R2 = (-1.0 / 12.0, 2.0 / 3.0, 5.0 / 12.0 - 1.0)
DIFF = (0.1, 0.05)
VM = pl.BlockSpec(memory_space=pltpu.VMEM)
SM = pl.BlockSpec(memory_space=pltpu.SMEM)


def flat(z, yh, chip, core):
    return (2 * chip + core) * 32 + (z % 16) * 2 + yh


def everyone():
    return [(z, yh, chip, core) for z in range(16) for yh in range(2)
            for chip in range(8) for core in range(2)]


def pair_groups():
    return [[flat(z, 0, c, k), flat(z, 1, c, k)] for z in range(16) for c in range(8) for k in range(2)]


def core_groups():
    return [[flat(z, h, c, 0), flat(z, h, c, 1)] for z in range(16) for h in range(2) for c in range(8)]


def z_pairs(step):
    return [(flat(z, h, c, k), flat(z + step, h, c, k)) for z, h, c, k in everyone()]


def split_pairs(step):
    return [(flat(z, h, c, k), flat(z + (step if k == 0 else -step), h, c, k))
            for z, h, c, k in everyone()]


def slice_pairs():
    return [(t * 32 + s, (t + 1) * 32 + s) for t in range(15) for s in range(32)]


def turn_groups(parity):
    groups = []
    for z, h, c, k in everyone():
        if c % 2 == parity:
            groups.append([flat(z, h, c, k), flat(z + (2 if k == 0 else -2), h, (c + 1) % 8, k)])
    return groups


def gather(x, groups):
    return lax.all_gather(x, AX, axis=0, axis_index_groups=groups, tiled=False)


def lane(x, n):
    return pltpu.roll(x, n % 128, x.ndim - 1)


def sub(x, n):
    return pltpu.roll(x, n % 8, x.ndim - 2)


def fine_lap(win, coef):
    n = win.shape[0] - 4
    mid = win[2:n + 2]
    near = win[1:n + 1] + win[3:n + 3]
    far = win[0:n] + win[4:n + 4]
    even = mid[:, 0]
    odd = mid[:, 1]
    even_up, even_dn = sub(even, 1), sub(even, -1)
    odd_up, odd_dn = sub(odd, 1), sub(odd, -1)
    nx = jnp.stack([odd + odd_up, even + even_dn], axis=1)
    fx = jnp.stack([even_up + even_dn, odd_up + odd_dn], axis=1)
    near = near + nx + (lane(mid, 1) + lane(mid, -1))
    far = far + fx + (lane(mid, 2) + lane(mid, -2))
    return (coef * 16.0 / 12.0) * near - (coef / 12.0) * far - (coef * 90.0 / 12.0) * mid


def coarse_lap(win, coef):
    n = win.shape[0] - 4
    mid = win[2:n + 2]
    near = win[1:n + 1] + win[3:n + 3] + (sub(mid, 1) + sub(mid, -1))
    far = win[0:n] + win[4:n + 4] + (sub(mid, 2) + sub(mid, -2))
    near_y = lane(mid, 1) + lane(mid, -1)
    far_y = lane(mid, 2) + lane(mid, -2)
    c = coef / 12.0
    return (4.0 * c) * near - (0.25 * c) * far + (16.0 * c) * near_y - c * far_y - (45.0 * c) * mid


def solve(bu, bv, g, ru, rv):
    u = (bu - g) * ru
    v = (bv + g) * rv
    g = u * v * v
    return (bu - g) * ru, (bv + g) * rv


def comb(w, xs):
    return w[0] * xs[0] + w[1] * xs[1] + w[2] * xs[2]


def pack_kernel(nv, st, fr, kr, out):
    for p in range(4):
        for par in range(2):
            rows = pl.ds(par, 8, stride=2)
            for j in range(3):
                for s in range(2):
                    out[p, 2 * j + s, par] = nv[0, j, s, p, rows, :]
            for s in range(2):
                out[p, 6 + s, par] = st[0, s, p, rows, :]
            out[p, 8, par] = fr[p, rows, :]
            out[p, 9, par] = kr[p, rows, :]


def first_combo(w, start):
    return start + (5.0 / 12.0 - 1.0) * w[0] + (2.0 / 3.0) * w[1] - (1.0 / 12.0) * w[2]


def sweep_kernel(pair, lo, hi, big, unit, aux, v1, v2, b2, xs, xp, cs):
    segs = ((lo, 2, 6), (pair, 8, 8), (hi, 16, 6))

    def raw(ref, i, f):
        if ref is pair:
            return ref[pl.ds(i, 2), f]
        return jnp.stack([ref[i * 10 + f], ref[i * 10 + 10 + f]])

    for s in range(2):
        v1[0, s] = lo[60 + s]
        v1[1, s] = lo[62 + s]
        v1[22, s] = hi[60 + s]
        v1[23, s] = hi[62 + s]

    for ref, base, count in segs:
        def load_v1(n, _, ref=ref, base=base):
            i = 2 * n
            for s in range(2):
                w = [raw(ref, i, 2 * j + s) for j in range(3)]
                start = raw(ref, i, 6 + s)
                v1[pl.ds(base + i, 2), s] = first_combo(w, start)
            return 0
        lax.fori_loop(0, count // 2, load_v1, 0)

    for ref, base, count in segs:
        def node_one(n, _, ref=ref, base=base):
            i = 2 * n
            p = base + i
            q = p - 2
            u = [raw(ref, i, 2 * j) for j in range(3)]
            v = [raw(ref, i, 2 * j + 1) for j in range(3)]
            su, sv = raw(ref, i, 6), raw(ref, i, 7)
            f = raw(ref, i, 8)
            fk = f + raw(ref, i, 9)
            ru = 1.0 / (1.0 + f)
            rv = 1.0 / (1.0 + fk)
            g = [u[j] * v[j] * v[j] for j in range(3)]
            gq = comb(R1, g)
            bu = su + f - f * comb(R1, u) - gq + fine_lap(v1[pl.ds(p - 2, 6), 0], DIFF[0])
            bv = sv + gq - fk * comb(R1, v) + fine_lap(v1[pl.ds(p - 2, 6), 1], DIFF[1])
            nu, nv = solve(bu, bv, g[1], ru, rv)
            at = pl.ds(q, 2)
            big[at, 0] = su
            big[at, 1] = sv
            big[at, 2] = nu
            big[at, 3] = nv
            big[at, 6] = f
            big[at, 7] = fk
            big[at, 8] = ru
            big[at, 9] = rv
            qu, qv = comb(R2, u), comb(R2, v)
            gq = comb(R2, g)
            v2[at, 0] = nu + qu + (u[2] - u[1])
            v2[at, 1] = nv + qv + (v[2] - v[1])
            b2[at, 0] = nu + f - f * qu - gq
            b2[at, 1] = nv + gq - fk * qv
            b2[at, 2] = g[2]
            return 0
        lax.fori_loop(0, count // 2, node_one, 0)

    def node_two(n, _):
        q = 2 + 2 * n
        at = pl.ds(q, 2)
        bu = b2[at, 0] + fine_lap(v2[pl.ds(q - 2, 6), 0], DIFF[0])
        bv = b2[at, 1] + fine_lap(v2[pl.ds(q - 2, 6), 1], DIFF[1])
        nu, nv = solve(bu, bv, b2[at, 2], big[at, 8], big[at, 9])
        big[at, 4] = nu
        big[at, 5] = nv
        return 0
    lax.fori_loop(0, 8, node_two, 0)

    def integrals(n, _):
        q = 4 + 2 * n
        at = pl.ds(q, 2)
        u = [big[at, 2 * j] for j in range(3)]
        v = [big[at, 2 * j + 1] for j in range(3)]
        f, fk = big[at, 6], big[at, 7]
        g = [u[j] * v[j] * v[j] for j in range(3)]
        to = pl.ds(2 * n, 2)
        for m, w in enumerate((W1, W2)):
            xu, xv, gx = comb(w, u), comb(w, v), comb(w, g)
            xs[to, 2 * m] = xu
            xs[to, 2 * m + 1] = xv
            xp[to, 2 * m] = f - f * xu - gx
            xp[to, 2 * m + 1] = gx - fk * xv
        return 0
    lax.fori_loop(0, 6, integrals, 0)

    def restrict(x):
        return 0.25 * (x[0, 0] + x[0, 1] + x[1, 0] + x[1, 1])

    def coarsen(n, _):
        at = pl.ds(2 * n, 2)
        for f in range(6):
            cs[n, f] = restrict(big[at, f])
        f = restrict(big[at, 6])
        k = restrict(big[at, 7])
        cs[n, 6] = f
        cs[n, 7] = k
        aux[n, 0] = cs[n, 0]
        aux[n, 1] = cs[n, 1]
        aux[n, 2] = 1.0 / (1.0 + f)
        aux[n, 3] = 1.0 / (1.0 + k)
        return 0
    lax.fori_loop(0, 10, coarsen, 0)

    def make_unit(n, _):
        for m in range(2):
            cu, cv = cs[3 + n, 2 * m + 2], cs[3 + n, 2 * m + 3]
            f, fk = cs[3 + n, 6], cs[3 + n, 7]
            g = cu * cv * cv
            for s in range(2):
                fl = fine_lap(xs[pl.ds(2 * n, 6), 2 * m + s], DIFF[s]) + xp[pl.ds(2 * n + 2, 2), 2 * m + s]
                val = restrict(fl) - coarse_lap(cs[pl.ds(n + 1, 5), 2 * m + s], DIFF[s])[0]
                if s == 0:
                    val = val + f * cu + g
                else:
                    val = val - g + fk * cv
                unit[n, 3 * m + s] = val
            unit[n, 3 * m + 2] = g
        return 0
    lax.fori_loop(0, 4, make_unit, 0)


def coarse_node(src, src_off, prm, prm_off, m, rates, rate_off, dst, dst_off, count):
    def step(n, _):
        i = 4 * n
        at = pl.ds(prm_off + i, 4)
        ra = pl.ds(rate_off + i, 4)
        wu = src[pl.ds(src_off + i, 8), 0]
        wv = src[pl.ds(src_off + i, 8), 1]
        bu = wu[2:6] + coarse_lap(wu, DIFF[0]) + prm[at, 3 * m]
        bv = wv[2:6] + coarse_lap(wv, DIFF[1]) + prm[at, 3 * m + 1]
        nu, nv = solve(bu, bv, prm[at, 3 * m + 2], rates[ra, 2], rates[ra, 3])
        dst[pl.ds(dst_off + i, 4), 0] = nu
        dst[pl.ds(dst_off + i, 4), 1] = nv
        return 0
    lax.fori_loop(0, count // 4, step, 0)


def two_slices(a, pa, pb, aux, n1, n2, n3, out):
    coarse_node(a, 0, pa, 0, 0, aux, 2, n1, 0, 28)
    coarse_node(n1, 0, pa, 2, 1, aux, 4, n2, 0, 24)
    coarse_node(n2, 0, pb, 0, 0, aux, 6, n3, 0, 20)
    coarse_node(n3, 0, pb, 2, 1, aux, 8, out, 0, 16)


def chain_kernel(a, pa, pb, aux, out, n1, n2, n3):
    two_slices(a, pa, pb, aux, n1, n2, n3, out)


def last_kernel(sc, a, pa, pb, aux, big, prev, res, n1, n2, n3, n4, gs, v1, tp):
    two_slices(a, pa, pb, aux, n1, n2, n3, n4)
    core = sc[0]
    yh = sc[1]

    @pl.when(core == 0)
    def _():
        for s in range(2):
            gs[:, s] = a[12:20, s]
            gs[:, 2 + s] = n1[10:18, s]
            gs[:, 4 + s] = n2[8:16, s]

    @pl.when(core != 0)
    def _():
        for s in range(2):
            gs[:, s] = n2[8:16, s]
            gs[:, 2 + s] = n3[6:14, s]
            gs[:, 4 + s] = n4[4:12, s]

    def restrict(x):
        return 0.25 * (x[0, 0] + x[0, 1] + x[1, 0] + x[1, 1])

    def update(i, _):
        row = 2 * yh + i
        at = pl.ds(2 + 4 * yh + 2 * i, 2)
        to = pl.ds(2 * i, 2)
        new = []
        for f in range(6):
            x = big[at, f]
            new.append(x + (gs[row, f] - restrict(x))[None, None])
        u, v = new[0::2], new[1::2]
        bu = prev[to, 0]
        bv = prev[to, 1]
        bu = bu + (gs[row, 0] - restrict(bu))[None, None]
        bv = bv + (gs[row, 1] - restrict(bv))[None, None]
        f, fk = big[at, 6], big[at, 7]
        g = [u[j] * v[j] * v[j] for j in range(3)]
        qu, qv, gq = comb(R1, u), comb(R1, v), comb(R1, g)
        v1[to, 0] = bu + qu + (u[1] - u[0])
        v1[to, 1] = bv + qv + (v[1] - v[0])
        tp[to, 0] = bu + f - f * qu - gq
        tp[to, 1] = bv + gq - fk * qv
        tp[to, 2] = g[1]
        qu, qv, gq = comb(R2, u), comb(R2, v), comb(R2, g)
        tp[to, 3] = qu + (u[2] - u[1])
        tp[to, 4] = qv + (v[2] - v[1])
        tp[to, 5] = f - f * qu - gq
        tp[to, 6] = gq - fk * qv
        tp[to, 7] = g[2]
        tp[to, 8] = bu
        tp[to, 9] = bv
        return 0
    lax.fori_loop(0, 6, update, 0)

    def put(node, s, plane, x):
        res[0, node, s, plane, pl.ds(0, 8, stride=2), :] = x[0]
        res[0, node, s, plane, pl.ds(1, 8, stride=2), :] = x[1]

    def node_one(n, _):
        i = 2 + 2 * n
        at = pl.ds(i, 2)
        br = pl.ds(2 + 4 * yh + i, 2)
        bu = tp[at, 0] + fine_lap(v1[pl.ds(i - 2, 6), 0], DIFF[0])
        bv = tp[at, 1] + fine_lap(v1[pl.ds(i - 2, 6), 1], DIFF[1])
        nu, nv = solve(bu, bv, tp[at, 2], big[br, 8], big[br, 9])
        tp[at, 3] = tp[at, 3] + nu
        tp[at, 4] = tp[at, 4] + nv
        tp[at, 5] = tp[at, 5] + nu
        tp[at, 6] = tp[at, 6] + nv
        tp[at, 10] = nu
        tp[at, 11] = nv
        return 0
    lax.fori_loop(0, 4, node_one, 0)

    for n in range(2):
        i = 4 + 2 * n
        at = pl.ds(i, 2)
        br = pl.ds(2 + 4 * yh + i, 2)
        bu = tp[at, 5] + fine_lap(tp[pl.ds(i - 2, 6), 3], DIFF[0])
        bv = tp[at, 6] + fine_lap(tp[pl.ds(i - 2, 6), 4], DIFF[1])
        nu, nv = solve(bu, bv, tp[at, 7], big[br, 8], big[br, 9])
        for d in range(2):
            p = 2 * n + d
            put(2, 0, p, nu[d])
            put(2, 1, p, nv[d])
            for s in range(2):
                put(0, s, p, tp[i + d, 8 + s])
                put(1, s, p, tp[i + d, 10 + s])


def vmem(*shape):
    return pltpu.VMEM(shape, F32)


def shape(*dims):
    return jax.ShapeDtypeStruct(dims, F32)


def body(node_values, start_state, feed_rate, kill_rate):
    t = lax.axis_index("tm")
    core = t % 2
    chip = t // 2
    yh = lax.axis_index("slab") % 2
    left = core == 0
    own = pl.pallas_call(
        pack_kernel, out_shape=shape(4, 10, 2, 8, 128), in_specs=[VM] * 4, out_specs=VM,
        name="pack",
    )(node_values, start_state, feed_rate, kill_rate)
    pair = gather(own, pair_groups()).reshape(8, 10, 2, 8, 128)

    def edge(planes, far):
        w = [far[:, 2 * j:2 * j + 2] for j in range(3)]
        v = first_combo(w, far[:, 6:8])
        return jnp.concatenate([planes.reshape(60, 2, 8, 128), v.reshape(4, 2, 8, 128)])

    lo = lax.ppermute(edge(pair[2:8], pair[0:2]), AX, z_pairs(1))
    hi = lax.ppermute(edge(pair[0:6], pair[6:8]), AX, z_pairs(-1))
    big, unit, aux = pl.pallas_call(
        sweep_kernel,
        out_shape=(shape(20, 10, 2, 8, 128), shape(4, 6, 8, 128), shape(10, 4, 8, 128)),
        in_specs=[VM] * 3, out_specs=(VM, VM, VM),
        scratch_shapes=[vmem(24, 2, 2, 8, 128), vmem(20, 2, 2, 8, 128), vmem(20, 3, 2, 8, 128),
                        vmem(12, 4, 2, 8, 128), vmem(12, 4, 2, 8, 128), vmem(10, 8, 8, 128)],
        name="sweep",
    )(pair, lo, hi)

    mine = lax.dynamic_slice_in_dim(big, 2 + 4 * yh, 12, 0)
    prev = lax.ppermute(mine[:, 4:6], AX, slice_pairs())
    prev = jnp.where(t == 0, mine[:, 0:2], prev)

    both = gather(jnp.concatenate([unit.reshape(24, 8, 128), aux.reshape(40, 8, 128)]), core_groups())
    units = both[:, :24].reshape(2, 4, 6, 8, 128)
    aux = both[0, 24:].reshape(10, 4, 8, 128)

    def send(parts, step):
        rows = [x.reshape(-1, 8, 128) for x in parts]
        return lax.ppermute(jnp.concatenate(rows), AX, split_pairs(step))

    got1 = send([units, jnp.where(left, aux[0:4], aux[6:10])], 1)
    aux1 = got1[48:].reshape(4, 4, 8, 128)
    got2 = send([units, got1[0:24],
                 jnp.where(left, jnp.concatenate([aux1[1:4], aux[0:4]]),
                           jnp.concatenate([aux[6:10], aux1[0:3]]))], 2)
    sides = gather(jnp.concatenate([got1, got2]), core_groups())

    def pick(side, start, planes, fields):
        return sides[side, start:start + planes * fields].reshape(planes, fields, 8, 128)

    pa = jnp.concatenate([pick(0, 64 + 48, 4, 6), pick(0, 64, 4, 6), pick(0, 0, 4, 6), units[0],
                          pick(1, 0, 4, 6), pick(1, 64, 4, 6), pick(1, 64 + 48, 4, 6)])
    pb = jnp.concatenate([pick(0, 64 + 24, 4, 6), pick(0, 24, 4, 6), units[1],
                          pick(1, 24, 4, 6), pick(1, 64 + 24, 4, 6)])
    aux = jnp.concatenate([pick(0, 64 + 72, 7, 4), pick(0, 48, 4, 4), aux,
                           pick(1, 48, 4, 4), pick(1, 64 + 72, 7, 4)])
    state = aux[:, 0:2]

    scratch = [vmem(28, 2, 8, 128), vmem(24, 2, 8, 128), vmem(20, 2, 8, 128)]
    for turn in range(7):
        out = pl.pallas_call(
            chain_kernel, out_shape=shape(16, 2, 8, 128), in_specs=[VM] * 4, out_specs=VM,
            scratch_shapes=scratch, name="chain",
        )(state, pa, pb, aux)
        moved = gather(out, turn_groups(turn % 2))[0]
        moved = gather(moved, core_groups()).reshape(32, 2, 8, 128)
        takes = jnp.logical_and(chip % 2 == (turn + 1) % 2, chip > 0)
        state = jnp.where(takes, moved, state)

    scalars = jnp.stack([core, yh]).astype(jnp.int32)
    return pl.pallas_call(
        last_kernel, out_shape=shape(1, 3, 2, 4, 16, 128), in_specs=[SM] + [VM] * 6, out_specs=VM,
        scratch_shapes=scratch + [vmem(16, 2, 8, 128), vmem(8, 6, 8, 128),
                                  vmem(12, 2, 2, 8, 128), vmem(12, 12, 2, 8, 128)],
        name="last",
    )(scalars, state, pa, pb, aux, big, prev)


def solution(mesh):
    return jax.shard_map(
        body,
        mesh=mesh,
        in_specs=(
            P("tm", None, None, "slab", None, None),
            P("tm", None, "slab", None, None),
            P("slab", None, None),
            P("slab", None, None),
        ),
        out_specs=P("tm", None, None, "slab", None, None),
        check_vma=False,
    )
```

```python
import jax
import jax.numpy as jnp
from jax import lax
from jax.experimental import pallas as pl
from jax.experimental.pallas import tpu as pltpu
from jax.sharding import PartitionSpec as P

AX = ("tm", "slab")
F32 = jnp.float32
W1 = (5.0 / 12.0, 2.0 / 3.0, -1.0 / 12.0)
W2 = (-1.0 / 12.0, 2.0 / 3.0, 5.0 / 12.0)
R1 = (5.0 / 12.0, 2.0 / 3.0 - 1.0, -1.0 / 12.0)
R2 = (-1.0 / 12.0, 2.0 / 3.0, 5.0 / 12.0 - 1.0)
DIFF = (0.1, 0.05)
VM = pl.BlockSpec(memory_space=pltpu.VMEM)
SM = pl.BlockSpec(memory_space=pltpu.SMEM)


def flat(z, yh, chip, core):
    return (2 * chip + core) * 32 + (z % 16) * 2 + yh


def everyone():
    return [(z, yh, chip, core) for z in range(16) for yh in range(2)
            for chip in range(8) for core in range(2)]


def pair_groups():
    return [[flat(z, 0, c, k), flat(z, 1, c, k)] for z in range(16) for c in range(8) for k in range(2)]


def core_groups():
    return [[flat(z, h, c, 0), flat(z, h, c, 1)] for z in range(16) for h in range(2) for c in range(8)]


def z_pairs(step):
    return [(flat(z, h, c, k), flat(z + step, h, c, k)) for z, h, c, k in everyone()]


def split_pairs(step):
    return [(flat(z, h, c, k), flat(z + (step if k == 0 else -step), h, c, k))
            for z, h, c, k in everyone()]


def slice_pairs():
    return [(t * 32 + s, (t + 1) * 32 + s) for t in range(15) for s in range(32)]


def turn_groups(parity):
    groups = []
    for z, h, c, k in everyone():
        if c % 2 == parity:
            groups.append([flat(z, h, c, k), flat(z + (2 if k == 0 else -2), h, (c + 1) % 8, k)])
    return groups


def gather(x, groups):
    return lax.all_gather(x, AX, axis=0, axis_index_groups=groups, tiled=False)


def lane(x, n):
    return pltpu.roll(x, n % 128, x.ndim - 1)


def sub(x, n):
    return pltpu.roll(x, n % 8, x.ndim - 2)


def fine_lap(win, coef):
    n = win.shape[0] - 4
    mid = win[2:n + 2]
    near = win[1:n + 1] + win[3:n + 3]
    far = win[0:n] + win[4:n + 4]
    even = mid[:, 0]
    odd = mid[:, 1]
    even_up, even_dn = sub(even, 1), sub(even, -1)
    odd_up, odd_dn = sub(odd, 1), sub(odd, -1)
    nx = jnp.stack([odd + odd_up, even + even_dn], axis=1)
    fx = jnp.stack([even_up + even_dn, odd_up + odd_dn], axis=1)
    near = near + nx + (lane(mid, 1) + lane(mid, -1))
    far = far + fx + (lane(mid, 2) + lane(mid, -2))
    return (coef * 16.0 / 12.0) * near - (coef / 12.0) * far - (coef * 90.0 / 12.0) * mid


def coarse_lap(win, coef):
    n = win.shape[0] - 4
    mid = win[2:n + 2]
    near = win[1:n + 1] + win[3:n + 3] + (sub(mid, 1) + sub(mid, -1))
    far = win[0:n] + win[4:n + 4] + (sub(mid, 2) + sub(mid, -2))
    near_y = lane(mid, 1) + lane(mid, -1)
    far_y = lane(mid, 2) + lane(mid, -2)
    c = coef / 12.0
    return (4.0 * c) * near - (0.25 * c) * far + (16.0 * c) * near_y - c * far_y - (45.0 * c) * mid


def solve(bu, bv, g, ru, rv):
    u = (bu - g) * ru
    v = (bv + g) * rv
    g = u * v * v
    return (bu - g) * ru, (bv + g) * rv


def comb(w, xs):
    return w[0] * xs[0] + w[1] * xs[1] + w[2] * xs[2]


def unrolled(count, step):
    for n in range(count):
        step(n, 0)


def pack_kernel(nv, st, fr, kr, out):
    for p in range(4):
        for par in range(2):
            rows = pl.ds(par, 8, stride=2)
            for j in range(3):
                for s in range(2):
                    out[p, 2 * j + s, par] = nv[0, j, s, p, rows, :]
            for s in range(2):
                out[p, 6 + s, par] = st[0, s, p, rows, :]
            out[p, 8, par] = fr[p, rows, :]
            out[p, 9, par] = kr[p, rows, :]


def first_combo(w, start):
    return start + (5.0 / 12.0 - 1.0) * w[0] + (2.0 / 3.0) * w[1] - (1.0 / 12.0) * w[2]


def sweep_kernel(pair, lo, hi, big, unit, aux, v1, v2, b2, xs, xp, cs):
    segs = ((lo, 2, 6), (pair, 8, 8), (hi, 16, 6))

    def raw(ref, i, f):
        if ref is pair:
            return ref[pl.ds(i, 2), f]
        return jnp.stack([ref[i * 10 + f], ref[i * 10 + 10 + f]])

    for s in range(2):
        v1[0, s] = lo[60 + s]
        v1[1, s] = lo[62 + s]
        v1[22, s] = hi[60 + s]
        v1[23, s] = hi[62 + s]

    for ref, base, count in segs:
        def load_v1(n, _, ref=ref, base=base):
            i = 2 * n
            for s in range(2):
                w = [raw(ref, i, 2 * j + s) for j in range(3)]
                start = raw(ref, i, 6 + s)
                v1[pl.ds(base + i, 2), s] = first_combo(w, start)
            return 0
        unrolled(count // 2, load_v1)

    for ref, base, count in segs:
        def node_one(n, _, ref=ref, base=base):
            i = 2 * n
            p = base + i
            q = p - 2
            u = [raw(ref, i, 2 * j) for j in range(3)]
            v = [raw(ref, i, 2 * j + 1) for j in range(3)]
            su, sv = raw(ref, i, 6), raw(ref, i, 7)
            f = raw(ref, i, 8)
            fk = f + raw(ref, i, 9)
            ru = 1.0 / (1.0 + f)
            rv = 1.0 / (1.0 + fk)
            g = [u[j] * v[j] * v[j] for j in range(3)]
            gq = comb(R1, g)
            bu = su + f - f * comb(R1, u) - gq + fine_lap(v1[pl.ds(p - 2, 6), 0], DIFF[0])
            bv = sv + gq - fk * comb(R1, v) + fine_lap(v1[pl.ds(p - 2, 6), 1], DIFF[1])
            nu, nv = solve(bu, bv, g[1], ru, rv)
            at = pl.ds(q, 2)
            big[at, 0] = su
            big[at, 1] = sv
            big[at, 2] = nu
            big[at, 3] = nv
            big[at, 6] = f
            big[at, 7] = fk
            big[at, 8] = ru
            big[at, 9] = rv
            qu, qv = comb(R2, u), comb(R2, v)
            gq = comb(R2, g)
            v2[at, 0] = nu + qu + (u[2] - u[1])
            v2[at, 1] = nv + qv + (v[2] - v[1])
            b2[at, 0] = nu + f - f * qu - gq
            b2[at, 1] = nv + gq - fk * qv
            b2[at, 2] = g[2]
            return 0
        unrolled(count // 2, node_one)

    def node_two(n, _):
        q = 2 + 2 * n
        at = pl.ds(q, 2)
        bu = b2[at, 0] + fine_lap(v2[pl.ds(q - 2, 6), 0], DIFF[0])
        bv = b2[at, 1] + fine_lap(v2[pl.ds(q - 2, 6), 1], DIFF[1])
        nu, nv = solve(bu, bv, b2[at, 2], big[at, 8], big[at, 9])
        big[at, 4] = nu
        big[at, 5] = nv
        return 0
    unrolled(8, node_two)

    def integrals(n, _):
        q = 4 + 2 * n
        at = pl.ds(q, 2)
        u = [big[at, 2 * j] for j in range(3)]
        v = [big[at, 2 * j + 1] for j in range(3)]
        f, fk = big[at, 6], big[at, 7]
        g = [u[j] * v[j] * v[j] for j in range(3)]
        to = pl.ds(2 * n, 2)
        for m, w in enumerate((W1, W2)):
            xu, xv, gx = comb(w, u), comb(w, v), comb(w, g)
            xs[to, 2 * m] = xu
            xs[to, 2 * m + 1] = xv
            xp[to, 2 * m] = f - f * xu - gx
            xp[to, 2 * m + 1] = gx - fk * xv
        return 0
    unrolled(6, integrals)

    def restrict(x):
        return 0.25 * (x[0, 0] + x[0, 1] + x[1, 0] + x[1, 1])

    def coarsen(n, _):
        at = pl.ds(2 * n, 2)
        for f in range(6):
            cs[n, f] = restrict(big[at, f])
        f = restrict(big[at, 6])
        k = restrict(big[at, 7])
        cs[n, 6] = f
        cs[n, 7] = k
        aux[n, 0] = cs[n, 0]
        aux[n, 1] = cs[n, 1]
        aux[n, 2] = 1.0 / (1.0 + f)
        aux[n, 3] = 1.0 / (1.0 + k)
        return 0
    unrolled(10, coarsen)

    def make_unit(n, _):
        for m in range(2):
            cu, cv = cs[3 + n, 2 * m + 2], cs[3 + n, 2 * m + 3]
            f, fk = cs[3 + n, 6], cs[3 + n, 7]
            g = cu * cv * cv
            for s in range(2):
                fl = fine_lap(xs[pl.ds(2 * n, 6), 2 * m + s], DIFF[s]) + xp[pl.ds(2 * n + 2, 2), 2 * m + s]
                val = restrict(fl) - coarse_lap(cs[pl.ds(n + 1, 5), 2 * m + s], DIFF[s])[0]
                if s == 0:
                    val = val + f * cu + g
                else:
                    val = val - g + fk * cv
                unit[n, 3 * m + s] = val
            unit[n, 3 * m + 2] = g
        return 0
    unrolled(4, make_unit)


def coarse_node(src, src_off, prm, prm_off, m, rates, rate_off, dst, dst_off, count):
    def step(n, _):
        i = 4 * n
        at = pl.ds(prm_off + i, 4)
        ra = pl.ds(rate_off + i, 4)
        wu = src[pl.ds(src_off + i, 8), 0]
        wv = src[pl.ds(src_off + i, 8), 1]
        bu = wu[2:6] + coarse_lap(wu, DIFF[0]) + prm[at, 3 * m]
        bv = wv[2:6] + coarse_lap(wv, DIFF[1]) + prm[at, 3 * m + 1]
        nu, nv = solve(bu, bv, prm[at, 3 * m + 2], rates[ra, 2], rates[ra, 3])
        dst[pl.ds(dst_off + i, 4), 0] = nu
        dst[pl.ds(dst_off + i, 4), 1] = nv
        return 0
    unrolled(count // 4, step)


def two_slices(a, pa, pb, aux, n1, n2, n3, out):
    coarse_node(a, 0, pa, 0, 0, aux, 2, n1, 0, 28)
    coarse_node(n1, 0, pa, 2, 1, aux, 4, n2, 0, 24)
    coarse_node(n2, 0, pb, 0, 0, aux, 6, n3, 0, 20)
    coarse_node(n3, 0, pb, 2, 1, aux, 8, out, 0, 16)


def take(flag, moved, a_in, a):
    @pl.when(flag != 0)
    def _():
        for side in range(2):
            a[pl.ds(16 * side, 16)] = moved[side]

    @pl.when(flag == 0)
    def _():
        a[...] = a_in[...]


def first_chain_kernel(a, pa, pb, aux, out, n1, n2, n3):
    two_slices(a, pa, pb, aux, n1, n2, n3, out)


def chain_kernel(sc, moved, a_in, pa, pb, aux, a, out, n1, n2, n3):
    take(sc[0], moved, a_in, a)
    two_slices(a, pa, pb, aux, n1, n2, n3, out)


def last_kernel(sc, moved, a_in, pa, pb, aux, big, prev, res, a, n1, n2, n3, n4, gs, v1, tp):
    take(sc[0], moved, a_in, a)
    two_slices(a, pa, pb, aux, n1, n2, n3, n4)
    core = sc[1]
    yh = sc[2]

    @pl.when(core == 0)
    def _():
        for s in range(2):
            gs[:, s] = a[12:20, s]
            gs[:, 2 + s] = n1[10:18, s]
            gs[:, 4 + s] = n2[8:16, s]

    @pl.when(core != 0)
    def _():
        for s in range(2):
            gs[:, s] = n2[8:16, s]
            gs[:, 2 + s] = n3[6:14, s]
            gs[:, 4 + s] = n4[4:12, s]

    def restrict(x):
        return 0.25 * (x[0, 0] + x[0, 1] + x[1, 0] + x[1, 1])

    def update(i, _):
        row = 2 * yh + i
        at = pl.ds(2 + 4 * yh + 2 * i, 2)
        to = pl.ds(2 * i, 2)
        new = []
        for f in range(6):
            x = big[at, f]
            new.append(x + (gs[row, f] - restrict(x))[None, None])
        u, v = new[0::2], new[1::2]
        bu = prev[to, 0]
        bv = prev[to, 1]
        bu = bu + (gs[row, 0] - restrict(bu))[None, None]
        bv = bv + (gs[row, 1] - restrict(bv))[None, None]
        f, fk = big[at, 6], big[at, 7]
        g = [u[j] * v[j] * v[j] for j in range(3)]
        qu, qv, gq = comb(R1, u), comb(R1, v), comb(R1, g)
        v1[to, 0] = bu + qu + (u[1] - u[0])
        v1[to, 1] = bv + qv + (v[1] - v[0])
        tp[to, 0] = bu + f - f * qu - gq
        tp[to, 1] = bv + gq - fk * qv
        tp[to, 2] = g[1]
        qu, qv, gq = comb(R2, u), comb(R2, v), comb(R2, g)
        tp[to, 3] = qu + (u[2] - u[1])
        tp[to, 4] = qv + (v[2] - v[1])
        tp[to, 5] = f - f * qu - gq
        tp[to, 6] = gq - fk * qv
        tp[to, 7] = g[2]
        tp[to, 8] = bu
        tp[to, 9] = bv
        return 0
    unrolled(6, update)

    def put(node, s, plane, x):
        res[0, node, s, plane, pl.ds(0, 8, stride=2), :] = x[0]
        res[0, node, s, plane, pl.ds(1, 8, stride=2), :] = x[1]

    def node_one(n, _):
        i = 2 + 2 * n
        at = pl.ds(i, 2)
        br = pl.ds(2 + 4 * yh + i, 2)
        bu = tp[at, 0] + fine_lap(v1[pl.ds(i - 2, 6), 0], DIFF[0])
        bv = tp[at, 1] + fine_lap(v1[pl.ds(i - 2, 6), 1], DIFF[1])
        nu, nv = solve(bu, bv, tp[at, 2], big[br, 8], big[br, 9])
        tp[at, 3] = tp[at, 3] + nu
        tp[at, 4] = tp[at, 4] + nv
        tp[at, 5] = tp[at, 5] + nu
        tp[at, 6] = tp[at, 6] + nv
        tp[at, 10] = nu
        tp[at, 11] = nv
        return 0
    unrolled(4, node_one)

    for n in range(2):
        i = 4 + 2 * n
        at = pl.ds(i, 2)
        br = pl.ds(2 + 4 * yh + i, 2)
        bu = tp[at, 5] + fine_lap(tp[pl.ds(i - 2, 6), 3], DIFF[0])
        bv = tp[at, 6] + fine_lap(tp[pl.ds(i - 2, 6), 4], DIFF[1])
        nu, nv = solve(bu, bv, tp[at, 7], big[br, 8], big[br, 9])
        for d in range(2):
            p = 2 * n + d
            put(2, 0, p, nu[d])
            put(2, 1, p, nv[d])
            for s in range(2):
                put(0, s, p, tp[i + d, 8 + s])
                put(1, s, p, tp[i + d, 10 + s])


def vmem(*shape):
    return pltpu.VMEM(shape, F32)


def shape(*dims):
    return jax.ShapeDtypeStruct(dims, F32)


def body(node_values, start_state, feed_rate, kill_rate):
    t = lax.axis_index("tm")
    core = t % 2
    chip = t // 2
    yh = lax.axis_index("slab") % 2
    left = core == 0
    own = pl.pallas_call(
        pack_kernel, out_shape=shape(4, 10, 2, 8, 128), in_specs=[VM] * 4, out_specs=VM,
        name="pack",
    )(node_values, start_state, feed_rate, kill_rate)
    pair = gather(own, pair_groups()).reshape(8, 10, 2, 8, 128)

    def edge(planes, far):
        w = [far[:, 2 * j:2 * j + 2] for j in range(3)]
        v = first_combo(w, far[:, 6:8])
        return jnp.concatenate([planes.reshape(60, 2, 8, 128), v.reshape(4, 2, 8, 128)])

    lo = lax.ppermute(edge(pair[2:8], pair[0:2]), AX, z_pairs(1))
    hi = lax.ppermute(edge(pair[0:6], pair[6:8]), AX, z_pairs(-1))
    big, unit, aux = pl.pallas_call(
        sweep_kernel,
        out_shape=(shape(20, 10, 2, 8, 128), shape(4, 6, 8, 128), shape(10, 4, 8, 128)),
        in_specs=[VM] * 3, out_specs=(VM, VM, VM),
        scratch_shapes=[vmem(24, 2, 2, 8, 128), vmem(20, 2, 2, 8, 128), vmem(20, 3, 2, 8, 128),
                        vmem(12, 4, 2, 8, 128), vmem(12, 4, 2, 8, 128), vmem(10, 8, 8, 128)],
        name="sweep",
    )(pair, lo, hi)

    mine = lax.dynamic_slice_in_dim(big, 2 + 4 * yh, 12, 0)
    prev = lax.ppermute(mine[:, 4:6], AX, slice_pairs())
    prev = jnp.where(t == 0, mine[:, 0:2], prev)

    both = gather(jnp.concatenate([unit.reshape(24, 8, 128), aux.reshape(40, 8, 128)]), core_groups())
    units = both[:, :24].reshape(2, 4, 6, 8, 128)
    aux = both[0, 24:].reshape(10, 4, 8, 128)

    def send(parts, step):
        rows = [x.reshape(-1, 8, 128) for x in parts]
        return lax.ppermute(jnp.concatenate(rows), AX, split_pairs(step))

    got1 = send([units, jnp.where(left, aux[0:4], aux[6:10])], 1)
    aux1 = got1[48:].reshape(4, 4, 8, 128)
    got2 = send([units, got1[0:24],
                 jnp.where(left, jnp.concatenate([aux1[1:4], aux[0:4]]),
                           jnp.concatenate([aux[6:10], aux1[0:3]]))], 2)
    near = gather(got1, core_groups())
    far = gather(got2[:48], core_groups())
    edge2 = gather(got2[48:], core_groups())

    def pick(rows, side, start, planes, fields):
        return rows[side, start:start + planes * fields].reshape(planes, fields, 8, 128)

    pa = jnp.concatenate([pick(edge2, 0, 0, 4, 6), pick(far, 0, 0, 4, 6), pick(near, 0, 0, 4, 6), units[0],
                          pick(near, 1, 0, 4, 6), pick(far, 1, 0, 4, 6), pick(edge2, 1, 0, 4, 6)])
    pb = jnp.concatenate([pick(far, 0, 24, 4, 6), pick(near, 0, 24, 4, 6), units[1],
                          pick(near, 1, 24, 4, 6), pick(far, 1, 24, 4, 6)])
    aux = jnp.concatenate([pick(edge2, 0, 24, 7, 4), pick(near, 0, 48, 4, 4), aux,
                           pick(near, 1, 48, 4, 4), pick(edge2, 1, 24, 7, 4)])
    state = aux[:, 0:2]

    scratch = [vmem(28, 2, 8, 128), vmem(24, 2, 8, 128), vmem(20, 2, 8, 128)]

    def exchange(out, turn):
        moved = gather(out, turn_groups(turn % 2))[0]
        moved = gather(moved, core_groups())
        takes = jnp.logical_and(chip % 2 == (turn + 1) % 2, chip > 0)
        return moved, takes.astype(jnp.int32)

    out = pl.pallas_call(
        first_chain_kernel, out_shape=shape(16, 2, 8, 128), in_specs=[VM] * 4, out_specs=VM,
        scratch_shapes=scratch, name="chain",
    )(state, pa, pb, aux)
    for turn in range(6):
        moved, takes = exchange(out, turn)
        state, out = pl.pallas_call(
            chain_kernel, out_shape=(shape(32, 2, 8, 128), shape(16, 2, 8, 128)),
            in_specs=[SM] + [VM] * 5, out_specs=(VM, VM),
            scratch_shapes=scratch, name="chain",
        )(takes.reshape(1), moved, state, pa, pb, aux)
    moved, takes = exchange(out, 6)

    scalars = jnp.stack([takes, core, yh]).astype(jnp.int32)
    return pl.pallas_call(
        last_kernel, out_shape=shape(1, 3, 2, 4, 16, 128), in_specs=[SM] + [VM] * 7, out_specs=VM,
        scratch_shapes=[vmem(32, 2, 8, 128)] + scratch + [vmem(16, 2, 8, 128), vmem(8, 6, 8, 128),
                                  vmem(12, 2, 2, 8, 128), vmem(12, 12, 2, 8, 128)],
        name="last",
    )(scalars, moved, state, pa, pb, aux, big, prev)


def solution(mesh):
    return jax.shard_map(
        body,
        mesh=mesh,
        in_specs=(
            P("tm", None, None, "slab", None, None),
            P("tm", None, "slab", None, None),
            P("slab", None, None),
            P("slab", None, None),
        ),
        out_specs=P("tm", None, None, "slab", None, None),
        check_vma=False,
    )
```

```python
import jax
import jax.numpy as jnp
from jax import lax
from jax.experimental import pallas as pl
from jax.experimental.pallas import tpu as pltpu
from jax.sharding import PartitionSpec as P

AX = ("tm", "slab")
F32 = jnp.float32
W1 = (5.0 / 12.0, 2.0 / 3.0, -1.0 / 12.0)
W2 = (-1.0 / 12.0, 2.0 / 3.0, 5.0 / 12.0)
R1 = (5.0 / 12.0, 2.0 / 3.0 - 1.0, -1.0 / 12.0)
R2 = (-1.0 / 12.0, 2.0 / 3.0, 5.0 / 12.0 - 1.0)
DIFF = (0.1, 0.05)
VM = pl.BlockSpec(memory_space=pltpu.VMEM)
SM = pl.BlockSpec(memory_space=pltpu.SMEM)
SMALL = pltpu.CompilerParams(vmem_limit_bytes=16 * 1024 * 1024)


def flat(z, yh, chip, core):
    return (2 * chip + core) * 32 + (z % 16) * 2 + yh


def everyone():
    return [(z, yh, chip, core) for z in range(16) for yh in range(2)
            for chip in range(8) for core in range(2)]


def pair_groups():
    return [[flat(z, 0, c, k), flat(z, 1, c, k)] for z in range(16) for c in range(8) for k in range(2)]


def core_groups():
    return [[flat(z, h, c, 0), flat(z, h, c, 1)] for z in range(16) for h in range(2) for c in range(8)]


def z_pairs(step):
    return [(flat(z, h, c, k), flat(z + step, h, c, k)) for z, h, c, k in everyone()]


def split_pairs(step):
    return [(flat(z, h, c, k), flat(z + (step if k == 0 else -step), h, c, k))
            for z, h, c, k in everyone()]


def slice_pairs():
    return [(t * 32 + s, (t + 1) * 32 + s) for t in range(15) for s in range(32)]


def turn_groups(parity):
    groups = []
    for z, h, c, k in everyone():
        if c % 2 == parity:
            groups.append([flat(z, h, c, k), flat(z + (2 if k == 0 else -2), h, (c + 1) % 8, k)])
    return groups


def gather(x, groups):
    return lax.all_gather(x, AX, axis=0, axis_index_groups=groups, tiled=False)


def lane(x, n):
    return pltpu.roll(x, n % 128, x.ndim - 1)


def sub(x, n):
    return pltpu.roll(x, n % 8, x.ndim - 2)


def fine_lap(win, coef):
    n = win.shape[0] - 4
    mid = win[2:n + 2]
    near = win[1:n + 1] + win[3:n + 3]
    far = win[0:n] + win[4:n + 4]
    even = mid[:, 0]
    odd = mid[:, 1]
    even_up, even_dn = sub(even, 1), sub(even, -1)
    odd_up, odd_dn = sub(odd, 1), sub(odd, -1)
    nx = jnp.stack([odd + odd_up, even + even_dn], axis=1)
    fx = jnp.stack([even_up + even_dn, odd_up + odd_dn], axis=1)
    near = near + nx + (lane(mid, 1) + lane(mid, -1))
    far = far + fx + (lane(mid, 2) + lane(mid, -2))
    return (coef * 16.0 / 12.0) * near - (coef / 12.0) * far - (coef * 90.0 / 12.0) * mid


def coarse_lap(win, coef):
    n = win.shape[0] - 4
    mid = win[2:n + 2]
    near = win[1:n + 1] + win[3:n + 3] + (sub(mid, 1) + sub(mid, -1))
    far = win[0:n] + win[4:n + 4] + (sub(mid, 2) + sub(mid, -2))
    near_y = lane(mid, 1) + lane(mid, -1)
    far_y = lane(mid, 2) + lane(mid, -2)
    c = coef / 12.0
    return (4.0 * c) * near - (0.25 * c) * far + (16.0 * c) * near_y - c * far_y - (45.0 * c) * mid


def solve(bu, bv, g, ru, rv):
    u = (bu - g) * ru
    v = (bv + g) * rv
    g = u * v * v
    return (bu - g) * ru, (bv + g) * rv


def comb(w, xs):
    return w[0] * xs[0] + w[1] * xs[1] + w[2] * xs[2]


def unrolled(count, step):
    for n in range(count):
        step(n, 0)


def pack_kernel(nv, st, fr, kr, out):
    for p in range(4):
        for par in range(2):
            rows = pl.ds(par, 8, stride=2)
            for j in range(3):
                for s in range(2):
                    out[p, 2 * j + s, par] = nv[0, j, s, p, rows, :]
            for s in range(2):
                out[p, 6 + s, par] = st[0, s, p, rows, :]
            out[p, 8, par] = fr[p, rows, :]
            out[p, 9, par] = kr[p, rows, :]


def first_combo(w, start):
    return start + (5.0 / 12.0 - 1.0) * w[0] + (2.0 / 3.0) * w[1] - (1.0 / 12.0) * w[2]


def sweep_kernel(pair, lo, hi, big, unit, aux, v1, v2, b2, xs, xp, cs):
    segs = ((lo, 2, 6), (pair, 8, 8), (hi, 16, 6))

    def raw(ref, i, f):
        if ref is pair:
            return ref[pl.ds(i, 2), f]
        return jnp.stack([ref[i * 10 + f], ref[i * 10 + 10 + f]])

    for s in range(2):
        v1[0, s] = lo[60 + s]
        v1[1, s] = lo[62 + s]
        v1[22, s] = hi[60 + s]
        v1[23, s] = hi[62 + s]

    for ref, base, count in segs:
        def load_v1(n, _, ref=ref, base=base):
            i = 2 * n
            for s in range(2):
                w = [raw(ref, i, 2 * j + s) for j in range(3)]
                start = raw(ref, i, 6 + s)
                v1[pl.ds(base + i, 2), s] = first_combo(w, start)
            return 0
        unrolled(count // 2, load_v1)

    for ref, base, count in segs:
        def node_one(n, _, ref=ref, base=base):
            i = 2 * n
            p = base + i
            q = p - 2
            u = [raw(ref, i, 2 * j) for j in range(3)]
            v = [raw(ref, i, 2 * j + 1) for j in range(3)]
            su, sv = raw(ref, i, 6), raw(ref, i, 7)
            f = raw(ref, i, 8)
            fk = f + raw(ref, i, 9)
            ru = 1.0 / (1.0 + f)
            rv = 1.0 / (1.0 + fk)
            g = [u[j] * v[j] * v[j] for j in range(3)]
            gq = comb(R1, g)
            bu = su + f - f * comb(R1, u) - gq + fine_lap(v1[pl.ds(p - 2, 6), 0], DIFF[0])
            bv = sv + gq - fk * comb(R1, v) + fine_lap(v1[pl.ds(p - 2, 6), 1], DIFF[1])
            nu, nv = solve(bu, bv, g[1], ru, rv)
            at = pl.ds(q, 2)
            big[at, 0] = su
            big[at, 1] = sv
            big[at, 2] = nu
            big[at, 3] = nv
            big[at, 6] = f
            big[at, 7] = fk
            big[at, 8] = ru
            big[at, 9] = rv
            qu, qv = comb(R2, u), comb(R2, v)
            gq = comb(R2, g)
            v2[at, 0] = nu + qu + (u[2] - u[1])
            v2[at, 1] = nv + qv + (v[2] - v[1])
            b2[at, 0] = nu + f - f * qu - gq
            b2[at, 1] = nv + gq - fk * qv
            b2[at, 2] = g[2]
            return 0
        unrolled(count // 2, node_one)

    def node_two(n, _):
        q = 2 + 2 * n
        at = pl.ds(q, 2)
        bu = b2[at, 0] + fine_lap(v2[pl.ds(q - 2, 6), 0], DIFF[0])
        bv = b2[at, 1] + fine_lap(v2[pl.ds(q - 2, 6), 1], DIFF[1])
        nu, nv = solve(bu, bv, b2[at, 2], big[at, 8], big[at, 9])
        big[at, 4] = nu
        big[at, 5] = nv
        return 0
    unrolled(8, node_two)

    def integrals(n, _):
        q = 4 + 2 * n
        at = pl.ds(q, 2)
        u = [big[at, 2 * j] for j in range(3)]
        v = [big[at, 2 * j + 1] for j in range(3)]
        f, fk = big[at, 6], big[at, 7]
        g = [u[j] * v[j] * v[j] for j in range(3)]
        to = pl.ds(2 * n, 2)
        for m, w in enumerate((W1, W2)):
            xu, xv, gx = comb(w, u), comb(w, v), comb(w, g)
            xs[to, 2 * m] = xu
            xs[to, 2 * m + 1] = xv
            xp[to, 2 * m] = f - f * xu - gx
            xp[to, 2 * m + 1] = gx - fk * xv
        return 0
    unrolled(6, integrals)

    def restrict(x):
        return 0.25 * (x[0, 0] + x[0, 1] + x[1, 0] + x[1, 1])

    def coarsen(n, _):
        at = pl.ds(2 * n, 2)
        for f in range(6):
            cs[n, f] = restrict(big[at, f])
        f = restrict(big[at, 6])
        k = restrict(big[at, 7])
        cs[n, 6] = f
        cs[n, 7] = k
        aux[n, 0] = cs[n, 0]
        aux[n, 1] = cs[n, 1]
        aux[n, 2] = 1.0 / (1.0 + f)
        aux[n, 3] = 1.0 / (1.0 + k)
        return 0
    unrolled(10, coarsen)

    def make_unit(n, _):
        for m in range(2):
            cu, cv = cs[3 + n, 2 * m + 2], cs[3 + n, 2 * m + 3]
            f, fk = cs[3 + n, 6], cs[3 + n, 7]
            g = cu * cv * cv
            for s in range(2):
                fl = fine_lap(xs[pl.ds(2 * n, 6), 2 * m + s], DIFF[s]) + xp[pl.ds(2 * n + 2, 2), 2 * m + s]
                val = restrict(fl) - coarse_lap(cs[pl.ds(n + 1, 5), 2 * m + s], DIFF[s])[0]
                if s == 0:
                    val = val + f * cu + g
                else:
                    val = val - g + fk * cv
                unit[n, 3 * m + s] = val
            unit[n, 3 * m + 2] = g
        return 0
    unrolled(4, make_unit)


def coarse_node(src, src_off, prm, prm_off, m, rates, rate_off, dst, dst_off, count):
    def step(n, _):
        i = 4 * n
        at = pl.ds(prm_off + i, 4)
        ra = pl.ds(rate_off + i, 4)
        wu = src[pl.ds(src_off + i, 8), 0]
        wv = src[pl.ds(src_off + i, 8), 1]
        bu = wu[2:6] + coarse_lap(wu, DIFF[0]) + prm[at, 3 * m]
        bv = wv[2:6] + coarse_lap(wv, DIFF[1]) + prm[at, 3 * m + 1]
        nu, nv = solve(bu, bv, prm[at, 3 * m + 2], rates[ra, 2], rates[ra, 3])
        dst[pl.ds(dst_off + i, 4), 0] = nu
        dst[pl.ds(dst_off + i, 4), 1] = nv
        return 0
    unrolled(count // 4, step)


def two_slices(a, pa, pb, aux, n1, n2, n3, out):
    coarse_node(a, 0, pa, 0, 0, aux, 2, n1, 0, 28)
    coarse_node(n1, 0, pa, 2, 1, aux, 4, n2, 0, 24)
    coarse_node(n2, 0, pb, 0, 0, aux, 6, n3, 0, 20)
    coarse_node(n3, 0, pb, 2, 1, aux, 8, out, 0, 16)


def take(flag, moved, a_in, a):
    @pl.when(flag != 0)
    def _():
        for side in range(2):
            a[pl.ds(16 * side, 16)] = moved[side]

    @pl.when(flag == 0)
    def _():
        a[...] = a_in[...]


def first_chain_kernel(a, pa, pb, aux, out, n1, n2, n3):
    two_slices(a, pa, pb, aux, n1, n2, n3, out)


def chain_kernel(sc, moved, a_in, pa, pb, aux, a, out, n1, n2, n3):
    take(sc[0], moved, a_in, a)
    two_slices(a, pa, pb, aux, n1, n2, n3, out)


def last_kernel(sc, moved, a_in, pa, pb, aux, big, prev, res, a, n1, n2, n3, n4, gs, v1, tp):
    take(sc[0], moved, a_in, a)
    two_slices(a, pa, pb, aux, n1, n2, n3, n4)
    core = sc[1]
    yh = sc[2]

    @pl.when(core == 0)
    def _():
        for s in range(2):
            gs[:, s] = a[12:20, s]
            gs[:, 2 + s] = n1[10:18, s]
            gs[:, 4 + s] = n2[8:16, s]

    @pl.when(core != 0)
    def _():
        for s in range(2):
            gs[:, s] = n2[8:16, s]
            gs[:, 2 + s] = n3[6:14, s]
            gs[:, 4 + s] = n4[4:12, s]

    def restrict(x):
        return 0.25 * (x[0, 0] + x[0, 1] + x[1, 0] + x[1, 1])

    def update(i, _):
        row = 2 * yh + i
        at = pl.ds(2 + 4 * yh + 2 * i, 2)
        to = pl.ds(2 * i, 2)
        new = []
        for f in range(6):
            x = big[at, f]
            new.append(x + (gs[row, f] - restrict(x))[None, None])
        u, v = new[0::2], new[1::2]
        bu = prev[to, 0]
        bv = prev[to, 1]
        bu = bu + (gs[row, 0] - restrict(bu))[None, None]
        bv = bv + (gs[row, 1] - restrict(bv))[None, None]
        f, fk = big[at, 6], big[at, 7]
        g = [u[j] * v[j] * v[j] for j in range(3)]
        qu, qv, gq = comb(R1, u), comb(R1, v), comb(R1, g)
        v1[to, 0] = bu + qu + (u[1] - u[0])
        v1[to, 1] = bv + qv + (v[1] - v[0])
        tp[to, 0] = bu + f - f * qu - gq
        tp[to, 1] = bv + gq - fk * qv
        tp[to, 2] = g[1]
        qu, qv, gq = comb(R2, u), comb(R2, v), comb(R2, g)
        tp[to, 3] = qu + (u[2] - u[1])
        tp[to, 4] = qv + (v[2] - v[1])
        tp[to, 5] = f - f * qu - gq
        tp[to, 6] = gq - fk * qv
        tp[to, 7] = g[2]
        tp[to, 8] = bu
        tp[to, 9] = bv
        return 0
    unrolled(6, update)

    def put(node, s, plane, x):
        res[0, node, s, plane, pl.ds(0, 8, stride=2), :] = x[0]
        res[0, node, s, plane, pl.ds(1, 8, stride=2), :] = x[1]

    def node_one(n, _):
        i = 2 + 2 * n
        at = pl.ds(i, 2)
        br = pl.ds(2 + 4 * yh + i, 2)
        bu = tp[at, 0] + fine_lap(v1[pl.ds(i - 2, 6), 0], DIFF[0])
        bv = tp[at, 1] + fine_lap(v1[pl.ds(i - 2, 6), 1], DIFF[1])
        nu, nv = solve(bu, bv, tp[at, 2], big[br, 8], big[br, 9])
        tp[at, 3] = tp[at, 3] + nu
        tp[at, 4] = tp[at, 4] + nv
        tp[at, 5] = tp[at, 5] + nu
        tp[at, 6] = tp[at, 6] + nv
        tp[at, 10] = nu
        tp[at, 11] = nv
        return 0
    unrolled(4, node_one)

    for n in range(2):
        i = 4 + 2 * n
        at = pl.ds(i, 2)
        br = pl.ds(2 + 4 * yh + i, 2)
        bu = tp[at, 5] + fine_lap(tp[pl.ds(i - 2, 6), 3], DIFF[0])
        bv = tp[at, 6] + fine_lap(tp[pl.ds(i - 2, 6), 4], DIFF[1])
        nu, nv = solve(bu, bv, tp[at, 7], big[br, 8], big[br, 9])
        for d in range(2):
            p = 2 * n + d
            put(2, 0, p, nu[d])
            put(2, 1, p, nv[d])
            for s in range(2):
                put(0, s, p, tp[i + d, 8 + s])
                put(1, s, p, tp[i + d, 10 + s])


def vmem(*shape):
    return pltpu.VMEM(shape, F32)


def shape(*dims):
    return jax.ShapeDtypeStruct(dims, F32)


def body(node_values, start_state, feed_rate, kill_rate):
    t = lax.axis_index("tm")
    core = t % 2
    chip = t // 2
    yh = lax.axis_index("slab") % 2
    left = core == 0
    own = pl.pallas_call(
        pack_kernel, out_shape=shape(4, 10, 2, 8, 128), in_specs=[VM] * 4, out_specs=VM,
        name="pack", compiler_params=SMALL,
    )(node_values, start_state, feed_rate, kill_rate)
    pair = gather(own, pair_groups()).reshape(8, 10, 2, 8, 128)

    def edge(planes, far):
        w = [far[:, 2 * j:2 * j + 2] for j in range(3)]
        v = first_combo(w, far[:, 6:8])
        return jnp.concatenate([planes.reshape(60, 2, 8, 128), v.reshape(4, 2, 8, 128)])

    lo = lax.ppermute(edge(pair[2:8], pair[0:2]), AX, z_pairs(1))
    hi = lax.ppermute(edge(pair[0:6], pair[6:8]), AX, z_pairs(-1))
    big, unit, aux = pl.pallas_call(
        sweep_kernel,
        out_shape=(shape(20, 10, 2, 8, 128), shape(4, 6, 8, 128), shape(10, 4, 8, 128)),
        in_specs=[VM] * 3, out_specs=(VM, VM, VM),
        scratch_shapes=[vmem(24, 2, 2, 8, 128), vmem(20, 2, 2, 8, 128), vmem(20, 3, 2, 8, 128),
                        vmem(12, 4, 2, 8, 128), vmem(12, 4, 2, 8, 128), vmem(10, 8, 8, 128)],
        name="sweep", compiler_params=SMALL,
    )(pair, lo, hi)

    mine = lax.dynamic_slice_in_dim(big, 2 + 4 * yh, 12, 0)
    prev = lax.ppermute(mine[:, 4:6], AX, slice_pairs())
    prev = jnp.where(t == 0, mine[:, 0:2], prev)

    both = gather(jnp.concatenate([unit.reshape(24, 8, 128), aux.reshape(40, 8, 128)]), core_groups())
    units = both[:, :24].reshape(2, 4, 6, 8, 128)
    aux = both[0, 24:].reshape(10, 4, 8, 128)

    def send(parts, step):
        rows = [x.reshape(-1, 8, 128) for x in parts]
        return lax.ppermute(jnp.concatenate(rows), AX, split_pairs(step))

    got1 = send([units, jnp.where(left, aux[0:4], aux[6:10])], 1)
    aux1 = got1[48:].reshape(4, 4, 8, 128)
    got2 = send([units, got1[0:24],
                 jnp.where(left, jnp.concatenate([aux1[1:4], aux[0:4]]),
                           jnp.concatenate([aux[6:10], aux1[0:3]]))], 2)
    near = gather(got1, core_groups())
    far = gather(got2[:48], core_groups())
    edge2 = gather(got2[48:], core_groups())

    def pick(rows, side, start, planes, fields):
        return rows[side, start:start + planes * fields].reshape(planes, fields, 8, 128)

    pa = jnp.concatenate([pick(edge2, 0, 0, 4, 6), pick(far, 0, 0, 4, 6), pick(near, 0, 0, 4, 6), units[0],
                          pick(near, 1, 0, 4, 6), pick(far, 1, 0, 4, 6), pick(edge2, 1, 0, 4, 6)])
    pb = jnp.concatenate([pick(far, 0, 24, 4, 6), pick(near, 0, 24, 4, 6), units[1],
                          pick(near, 1, 24, 4, 6), pick(far, 1, 24, 4, 6)])
    aux = jnp.concatenate([pick(edge2, 0, 24, 7, 4), pick(near, 0, 48, 4, 4), aux,
                           pick(near, 1, 48, 4, 4), pick(edge2, 1, 24, 7, 4)])
    state = aux[:, 0:2]

    scratch = [vmem(28, 2, 8, 128), vmem(24, 2, 8, 128), vmem(20, 2, 8, 128)]

    def exchange(out, turn):
        moved = gather(out, turn_groups(turn % 2))[0]
        moved = gather(moved, core_groups())
        takes = jnp.logical_and(chip % 2 == (turn + 1) % 2, chip > 0)
        return moved, takes.astype(jnp.int32)

    out = pl.pallas_call(
        first_chain_kernel, out_shape=shape(16, 2, 8, 128), in_specs=[VM] * 4, out_specs=VM,
        scratch_shapes=scratch, name="chain", compiler_params=SMALL,
    )(state, pa, pb, aux)
    for turn in range(6):
        moved, takes = exchange(out, turn)
        state, out = pl.pallas_call(
            chain_kernel, out_shape=(shape(32, 2, 8, 128), shape(16, 2, 8, 128)),
            in_specs=[SM] + [VM] * 5, out_specs=(VM, VM),
            scratch_shapes=scratch, name="chain", compiler_params=SMALL,
        )(takes.reshape(1), moved, state, pa, pb, aux)
    moved, takes = exchange(out, 6)

    scalars = jnp.stack([takes, core, yh]).astype(jnp.int32)
    return pl.pallas_call(
        last_kernel, out_shape=shape(1, 3, 2, 4, 16, 128), in_specs=[SM] + [VM] * 7, out_specs=VM,
        scratch_shapes=[vmem(32, 2, 8, 128)] + scratch + [vmem(16, 2, 8, 128), vmem(8, 6, 8, 128),
                                  vmem(12, 2, 2, 8, 128), vmem(12, 12, 2, 8, 128)],
        name="last", compiler_params=SMALL,
    )(scalars, moved, state, pa, pb, aux, big, prev)


def solution(mesh):
    return jax.shard_map(
        body,
        mesh=mesh,
        in_specs=(
            P("tm", None, None, "slab", None, None),
            P("tm", None, "slab", None, None),
            P("slab", None, None),
            P("slab", None, None),
        ),
        out_specs=P("tm", None, None, "slab", None, None),
        check_vma=False,
    )
```

```python
import jax
import jax.numpy as jnp
from jax import lax
from jax.experimental import pallas as pl
from jax.experimental.pallas import tpu as pltpu
from jax.sharding import PartitionSpec as P


AX = ("tm", "slab")
F32 = jnp.float32
W1 = (5.0 / 12.0, 2.0 / 3.0, -1.0 / 12.0)
W2 = (-1.0 / 12.0, 2.0 / 3.0, 5.0 / 12.0)
R1 = (5.0 / 12.0, 2.0 / 3.0 - 1.0, -1.0 / 12.0)
R2 = (-1.0 / 12.0, 2.0 / 3.0, 5.0 / 12.0 - 1.0)
DIFF = (0.1, 0.05)
VM = pl.BlockSpec(memory_space=pltpu.VMEM)
SM = pl.BlockSpec(memory_space=pltpu.SMEM)
SMALL = pltpu.CompilerParams(vmem_limit_bytes=16 * 1024 * 1024)


def flat(z, yh, chip, core):
    return (2 * chip + core) * 32 + (z % 16) * 2 + yh


def everyone():
    return [(z, yh, chip, core) for z in range(16) for yh in range(2)
            for chip in range(8) for core in range(2)]


def pair_groups():
    return [[flat(z, 0, c, k), flat(z, 1, c, k)] for z in range(16) for c in range(8) for k in range(2)]


def core_groups():
    return [[flat(z, h, c, 0), flat(z, h, c, 1)] for z in range(16) for h in range(2) for c in range(8)]


def z_pairs(step):
    return [(flat(z, h, c, k), flat(z + step, h, c, k)) for z, h, c, k in everyone()]


def split_pairs(step):
    return [(flat(z, h, c, k), flat(z + (step if k == 0 else -step), h, c, k))
            for z, h, c, k in everyone()]


def slice_pairs():
    return [(t * 32 + s, (t + 1) * 32 + s) for t in range(15) for s in range(32)]


def turn_pairs(turn):
    return [(flat(z, h, turn, k), flat(z + (2 if k == 0 else -2), h, turn + 1, k))
            for z in range(16) for h in range(2) for k in range(2)]


def gather(x, groups):
    return lax.all_gather(x, AX, axis=0, axis_index_groups=groups, tiled=False)


def lane(x, n):
    return pltpu.roll(x, n % 128, x.ndim - 1)


def sub(x, n):
    return pltpu.roll(x, n % 8, x.ndim - 2)


def fine_lap(win, coef):
    n = win.shape[0] - 4
    mid = win[2:n + 2]
    near = win[1:n + 1] + win[3:n + 3]
    far = win[0:n] + win[4:n + 4]
    even = mid[:, 0]
    odd = mid[:, 1]
    even_up, even_dn = sub(even, 1), sub(even, -1)
    odd_up, odd_dn = sub(odd, 1), sub(odd, -1)
    nx = jnp.stack([odd + odd_up, even + even_dn], axis=1)
    fx = jnp.stack([even_up + even_dn, odd_up + odd_dn], axis=1)
    near = near + nx + (lane(mid, 1) + lane(mid, -1))
    far = far + fx + (lane(mid, 2) + lane(mid, -2))
    return (coef * 16.0 / 12.0) * near - (coef / 12.0) * far - (coef * 90.0 / 12.0) * mid


def coarse_lap(win, coef):
    n = win.shape[0] - 4
    mid = win[2:n + 2]
    near = win[1:n + 1] + win[3:n + 3] + (sub(mid, 1) + sub(mid, -1))
    far = win[0:n] + win[4:n + 4] + (sub(mid, 2) + sub(mid, -2))
    near_y = lane(mid, 1) + lane(mid, -1)
    far_y = lane(mid, 2) + lane(mid, -2)
    c = coef / 12.0
    return (4.0 * c) * near - (0.25 * c) * far + (16.0 * c) * near_y - c * far_y - (45.0 * c) * mid


def solve(bu, bv, g, ru, rv):
    u = (bu - g) * ru
    v = (bv + g) * rv
    g = u * v * v
    return (bu - g) * ru, (bv + g) * rv


def comb(w, xs):
    return w[0] * xs[0] + w[1] * xs[1] + w[2] * xs[2]


def unrolled(count, step):
    for n in range(count):
        step(n, 0)


def pack_kernel(nv, st, fr, kr, out):
    for p in range(4):
        for par in range(2):
            rows = pl.ds(par, 8, stride=2)
            for j in range(3):
                for s in range(2):
                    out[p, 2 * j + s, par] = nv[0, j, s, p, rows, :]
            for s in range(2):
                out[p, 6 + s, par] = st[0, s, p, rows, :]
            out[p, 8, par] = fr[p, rows, :]
            out[p, 9, par] = kr[p, rows, :]


def first_combo(w, start):
    return start + (5.0 / 12.0 - 1.0) * w[0] + (2.0 / 3.0) * w[1] - (1.0 / 12.0) * w[2]


def sweep_kernel(pair, lo, hi, big, unit, start, rates, v1, v2, b2, xs, xp, cs):
    segs = ((lo, 2, 6), (pair, 8, 8), (hi, 16, 6))

    def raw(ref, i, f):
        if ref is pair:
            return ref[pl.ds(i, 2), f]
        return jnp.stack([ref[i * 10 + f], ref[i * 10 + 10 + f]])

    for s in range(2):
        v1[0, s] = lo[60 + s]
        v1[1, s] = lo[62 + s]
        v1[22, s] = hi[60 + s]
        v1[23, s] = hi[62 + s]

    for ref, base, count in segs:
        def load_v1(n, _, ref=ref, base=base):
            i = 2 * n
            for s in range(2):
                w = [raw(ref, i, 2 * j + s) for j in range(3)]
                start = raw(ref, i, 6 + s)
                v1[pl.ds(base + i, 2), s] = first_combo(w, start)
            return 0

        unrolled(count // 2, load_v1)

    for ref, base, count in segs:
        def node_one(n, _, ref=ref, base=base):
            i = 2 * n
            p = base + i
            q = p - 2
            u = [raw(ref, i, 2 * j) for j in range(3)]
            v = [raw(ref, i, 2 * j + 1) for j in range(3)]
            su, sv = raw(ref, i, 6), raw(ref, i, 7)
            f = raw(ref, i, 8)
            fk = f + raw(ref, i, 9)
            ru = 1.0 / (1.0 + f)
            rv = 1.0 / (1.0 + fk)
            g = [u[j] * v[j] * v[j] for j in range(3)]
            gq = comb(R1, g)
            bu = su + f - f * comb(R1, u) - gq + fine_lap(v1[pl.ds(p - 2, 6), 0], DIFF[0])
            bv = sv + gq - fk * comb(R1, v) + fine_lap(v1[pl.ds(p - 2, 6), 1], DIFF[1])
            nu, nv = solve(bu, bv, g[1], ru, rv)
            at = pl.ds(q, 2)
            big[at, 0] = su
            big[at, 1] = sv
            big[at, 2] = nu
            big[at, 3] = nv
            big[at, 6] = f
            big[at, 7] = fk
            big[at, 8] = ru
            big[at, 9] = rv
            qu, qv = comb(R2, u), comb(R2, v)
            gq = comb(R2, g)
            v2[at, 0] = nu + qu + (u[2] - u[1])
            v2[at, 1] = nv + qv + (v[2] - v[1])
            b2[at, 0] = nu + f - f * qu - gq
            b2[at, 1] = nv + gq - fk * qv
            b2[at, 2] = g[2]
            return 0

        unrolled(count // 2, node_one)

    def node_two(n, _):
        q = 2 + 2 * n
        at = pl.ds(q, 2)
        bu = b2[at, 0] + fine_lap(v2[pl.ds(q - 2, 6), 0], DIFF[0])
        bv = b2[at, 1] + fine_lap(v2[pl.ds(q - 2, 6), 1], DIFF[1])
        nu, nv = solve(bu, bv, b2[at, 2], big[at, 8], big[at, 9])
        big[at, 4] = nu
        big[at, 5] = nv
        return 0

    unrolled(8, node_two)

    def integrals(n, _):
        q = 4 + 2 * n
        at = pl.ds(q, 2)
        u = [big[at, 2 * j] for j in range(3)]
        v = [big[at, 2 * j + 1] for j in range(3)]
        f, fk = big[at, 6], big[at, 7]
        g = [u[j] * v[j] * v[j] for j in range(3)]
        to = pl.ds(2 * n, 2)
        for m, w in enumerate((W1, W2)):
            xu, xv, gx = comb(w, u), comb(w, v), comb(w, g)
            xs[to, 2 * m] = xu
            xs[to, 2 * m + 1] = xv
            xp[to, 2 * m] = f - f * xu - gx
            xp[to, 2 * m + 1] = gx - fk * xv
        return 0

    unrolled(6, integrals)

    def restrict(x):
        return 0.25 * (x[0, 0] + x[0, 1] + x[1, 0] + x[1, 1])

    def coarsen(n, _):
        at = pl.ds(2 * n, 2)
        for f in range(6):
            cs[n, f] = restrict(big[at, f])
        f = restrict(big[at, 6])
        k = restrict(big[at, 7])
        cs[n, 6] = f
        cs[n, 7] = k
        start[n, 0] = cs[n, 0]
        start[n, 1] = cs[n, 1]
        rates[n, 0] = 1.0 / (1.0 + f)
        rates[n, 1] = 1.0 / (1.0 + k)
        return 0

    unrolled(10, coarsen)

    def make_unit(n, _):
        for m in range(2):
            cu, cv = cs[3 + n, 2 * m + 2], cs[3 + n, 2 * m + 3]
            f, fk = cs[3 + n, 6], cs[3 + n, 7]
            g = cu * cv * cv
            for s in range(2):
                fl = fine_lap(xs[pl.ds(2 * n, 6), 2 * m + s], DIFF[s]) + xp[pl.ds(2 * n + 2, 2), 2 * m + s]
                val = restrict(fl) - coarse_lap(cs[pl.ds(n + 1, 5), 2 * m + s], DIFF[s])[0]
                if s == 0:
                    val = val + f * cu + g
                else:
                    val = val - g + fk * cv
                unit[m, n, s] = val
            unit[m, n, 2] = g
        return 0

    unrolled(4, make_unit)


def coarse_node(src, prm, rates, rate_off, dst, count):
    def step(n, _):
        i = 4 * n
        at = pl.ds(i, 4)
        ra = pl.ds(rate_off + i, 4)
        wu = src[pl.ds(i, 8), 0]
        wv = src[pl.ds(i, 8), 1]
        bu = wu[2:6] + coarse_lap(wu, DIFF[0]) + prm[at, 0]
        bv = wv[2:6] + coarse_lap(wv, DIFF[1]) + prm[at, 1]
        nu, nv = solve(bu, bv, prm[at, 2], rates[ra, 0], rates[ra, 1])
        dst[at, 0] = nu
        dst[at, 1] = nv

    unrolled(count // 4, step)


def two_slices(a, prm, n1, n2, n3, out):
    p1a, p2a, p1b, p2b, rates = prm
    coarse_node(a, p1a, rates, 0, n1, 28)
    coarse_node(n1, p2a, rates, 2, n2, 24)
    coarse_node(n2, p1b, rates, 4, n3, 20)
    coarse_node(n3, p2b, rates, 6, out, 16)


def take(flag, moved, a_in, a):
    @pl.when(flag != 0)
    def _():
        for side in range(2):
            a[pl.ds(16 * side, 16)] = moved[side]

    @pl.when(flag == 0)
    def _():
        a[...] = a_in[...]


def first_chain_kernel(a, p1a, p2a, p1b, p2b, rates, out, n1, n2, n3):
    two_slices(a, (p1a, p2a, p1b, p2b, rates), n1, n2, n3, out)


def chain_kernel(sc, moved, a_in, p1a, p2a, p1b, p2b, rates, a, out, n1, n2, n3):
    take(sc[0], moved, a_in, a)
    two_slices(a, (p1a, p2a, p1b, p2b, rates), n1, n2, n3, out)


def last_kernel(sc, moved, a_in, p1a, p2a, p1b, p2b, rates, big, prev, res, a, n1, n2, n3, n4, gs, v1, tp):
    take(sc[0], moved, a_in, a)
    two_slices(a, (p1a, p2a, p1b, p2b, rates), n1, n2, n3, n4)
    core = sc[1]
    yh = sc[2]

    @pl.when(core == 0)
    def _():
        for s in range(2):
            gs[:, s] = a[12:20, s]
            gs[:, 2 + s] = n1[10:18, s]
            gs[:, 4 + s] = n2[8:16, s]

    @pl.when(core != 0)
    def _():
        for s in range(2):
            gs[:, s] = n2[8:16, s]
            gs[:, 2 + s] = n3[6:14, s]
            gs[:, 4 + s] = n4[4:12, s]

    def restrict(x):
        return 0.25 * (x[0, 0] + x[0, 1] + x[1, 0] + x[1, 1])

    def update(i, _):
        row = 2 * yh + i
        at = pl.ds(2 + 4 * yh + 2 * i, 2)
        to = pl.ds(2 * i, 2)
        new = []
        for f in range(6):
            x = big[at, f]
            new.append(x + (gs[row, f] - restrict(x))[None, None])
        u, v = new[0::2], new[1::2]
        bu = prev[to, 0]
        bv = prev[to, 1]
        bu = bu + (gs[row, 0] - restrict(bu))[None, None]
        bv = bv + (gs[row, 1] - restrict(bv))[None, None]
        f, fk = big[at, 6], big[at, 7]
        g = [u[j] * v[j] * v[j] for j in range(3)]
        qu, qv, gq = comb(R1, u), comb(R1, v), comb(R1, g)
        v1[to, 0] = bu + qu + (u[1] - u[0])
        v1[to, 1] = bv + qv + (v[1] - v[0])
        tp[to, 0] = bu + f - f * qu - gq
        tp[to, 1] = bv + gq - fk * qv
        tp[to, 2] = g[1]
        qu, qv, gq = comb(R2, u), comb(R2, v), comb(R2, g)
        tp[to, 3] = qu + (u[2] - u[1])
        tp[to, 4] = qv + (v[2] - v[1])
        tp[to, 5] = f - f * qu - gq
        tp[to, 6] = gq - fk * qv
        tp[to, 7] = g[2]
        tp[to, 8] = bu
        tp[to, 9] = bv
        return 0

    unrolled(6, update)

    def put(node, s, plane, x):
        res[0, node, s, plane, pl.ds(0, 8, stride=2), :] = x[0]
        res[0, node, s, plane, pl.ds(1, 8, stride=2), :] = x[1]

    def node_one(n, _):
        i = 2 + 2 * n
        at = pl.ds(i, 2)
        br = pl.ds(2 + 4 * yh + i, 2)
        bu = tp[at, 0] + fine_lap(v1[pl.ds(i - 2, 6), 0], DIFF[0])
        bv = tp[at, 1] + fine_lap(v1[pl.ds(i - 2, 6), 1], DIFF[1])
        nu, nv = solve(bu, bv, tp[at, 2], big[br, 8], big[br, 9])
        tp[at, 3] = tp[at, 3] + nu
        tp[at, 4] = tp[at, 4] + nv
        tp[at, 5] = tp[at, 5] + nu
        tp[at, 6] = tp[at, 6] + nv
        tp[at, 10] = nu
        tp[at, 11] = nv
        return 0

    unrolled(4, node_one)

    for n in range(2):
        i = 4 + 2 * n
        at = pl.ds(i, 2)
        br = pl.ds(2 + 4 * yh + i, 2)
        bu = tp[at, 5] + fine_lap(tp[pl.ds(i - 2, 6), 3], DIFF[0])
        bv = tp[at, 6] + fine_lap(tp[pl.ds(i - 2, 6), 4], DIFF[1])
        nu, nv = solve(bu, bv, tp[at, 7], big[br, 8], big[br, 9])
        for d in range(2):
            p = 2 * n + d
            put(2, 0, p, nu[d])
            put(2, 1, p, nv[d])
            for s in range(2):
                put(0, s, p, tp[i + d, 8 + s])
                put(1, s, p, tp[i + d, 10 + s])


def vmem(*shape):
    return pltpu.VMEM(shape, F32)


def shape(*dims):
    return jax.ShapeDtypeStruct(dims, F32)


def program(node_values, start_state, feed_rate, kill_rate):
    t = lax.axis_index("tm")
    core = t % 2
    chip = t // 2
    yh = lax.axis_index("slab") % 2
    left = core == 0
    own = pl.pallas_call(
        pack_kernel, out_shape=shape(4, 10, 2, 8, 128), in_specs=[VM] * 4, out_specs=VM,
        name="pack",
    )(node_values, start_state, feed_rate, kill_rate)
    pair = gather(own, pair_groups()).reshape(8, 10, 2, 8, 128)

    def edge(planes, far):
        w = [far[:, 2 * j:2 * j + 2] for j in range(3)]
        v = first_combo(w, far[:, 6:8])
        return jnp.concatenate([planes.reshape(60, 2, 8, 128), v.reshape(4, 2, 8, 128)])

    lo = lax.ppermute(edge(pair[2:8], pair[0:2]), AX, z_pairs(1))
    hi = lax.ppermute(edge(pair[0:6], pair[6:8]), AX, z_pairs(-1))
    big, unit, start, rates = pl.pallas_call(
        sweep_kernel,
        out_shape=(shape(20, 10, 2, 8, 128), shape(2, 4, 3, 8, 128), shape(10, 2, 8, 128),
                   shape(10, 2, 8, 128)),
        in_specs=[VM] * 3, out_specs=(VM, VM, VM, VM),
        scratch_shapes=[vmem(24, 2, 2, 8, 128), vmem(20, 2, 2, 8, 128), vmem(20, 3, 2, 8, 128),
                        vmem(12, 4, 2, 8, 128), vmem(12, 4, 2, 8, 128), vmem(10, 8, 8, 128)],
        name="sweep", compiler_params=SMALL,
    )(pair, lo, hi)

    def rows(parts):
        return jnp.concatenate([x.reshape(-1, 8, 128) for x in parts])

    both = gather(rows([unit, start]), core_groups())
    units = both[:, :24].reshape(2, 2, 4, 3, 8, 128)
    start = both[0, 24:].reshape(10, 2, 8, 128)
    (p1a, p2a), (p1b, p2b) = units

    def near_planes(x, n):
        return jnp.where(left, x[4 - n:], x[:n])

    def send(parts, step):
        message = rows(parts)
        return lax.ppermute(message, AX, split_pairs(step))

    start4 = jnp.where(left, start[0:4], start[6:10])
    rates4 = jnp.where(left, rates[0:4], rates[6:10])
    near = send([p1a, p2a, p1b, p2b, start4, rates4], 1)
    mid = send([p1a, p2a, p1b, near_planes(p2b, 2), start4, rates4], 2)
    far = send([p1a, near_planes(p2a, 2), jnp.where(left, start[1:4], start[6:9]),
                jnp.where(left, rates[3:4], rates[6:7])], 3)
    nears = gather(near, core_groups())
    fars = gather(jnp.concatenate([mid, far]), core_groups())

    def pick(part, side, first, planes, fields):
        return part[side, first:first + planes * fields].reshape(planes, fields, 8, 128)

    def window(own, *pieces):
        below = [pick(part, 0, first, planes, own.shape[1]) for part, first, planes in pieces]
        above = [pick(part, 1, first, planes, own.shape[1]) for part, first, planes in pieces]
        return jnp.concatenate(below[::-1] + [own] + above)

    p1a = window(p1a, (nears, 0, 4), (fars, 0, 4), (fars, 58, 4))
    p2a = window(p2a, (nears, 12, 4), (fars, 12, 4), (fars, 70, 2))
    p1b = window(p1b, (nears, 24, 4), (fars, 24, 4))
    p2b = window(p2b, (nears, 36, 4), (fars, 36, 2))
    state = window(start, (nears, 48, 4), (fars, 42, 4), (fars, 76, 3))
    rates = window(rates, (nears, 56, 4), (fars, 50, 4), (fars, 82, 1))
    prm = (p1a, p2a, p1b, p2b, rates)

    mine = lax.dynamic_slice_in_dim(big, 2 + 4 * yh, 12, 0)
    prev = lax.ppermute(mine[:, 4:6], AX, slice_pairs())
    prev = jnp.where(t == 0, mine[:, 0:2], prev)

    scratch = [vmem(28, 2, 8, 128), vmem(24, 2, 8, 128), vmem(20, 2, 8, 128)]

    def exchange(out, turn):
        moved = lax.ppermute(out, AX, turn_pairs(turn))
        moved = gather(moved, core_groups())
        return moved, (chip == turn + 1).astype(jnp.int32)

    out = pl.pallas_call(
        first_chain_kernel, out_shape=shape(16, 2, 8, 128), in_specs=[VM] * 6, out_specs=VM,
        scratch_shapes=scratch, name="chain", compiler_params=SMALL,
    )(state, *prm)
    for turn in range(6):
        moved, takes = exchange(out, turn)
        state, out = pl.pallas_call(
            chain_kernel, out_shape=(shape(32, 2, 8, 128), shape(16, 2, 8, 128)),
            in_specs=[SM] + [VM] * 7, out_specs=(VM, VM),
            scratch_shapes=scratch, name="chain", compiler_params=SMALL,
        )(takes.reshape(1), moved, state, *prm)
    moved, takes = exchange(out, 6)

    scalars = jnp.stack([takes, core, yh]).astype(jnp.int32)
    return pl.pallas_call(
        last_kernel, out_shape=shape(1, 3, 2, 4, 16, 128), in_specs=[SM] + [VM] * 9, out_specs=VM,
        scratch_shapes=[vmem(32, 2, 8, 128)] + scratch + [
            vmem(16, 2, 8, 128), vmem(8, 6, 8, 128), vmem(12, 2, 2, 8, 128), vmem(12, 12, 2, 8, 128)],
        name="last", compiler_params=SMALL,
    )(scalars, moved, state, *prm, big, prev)


def solution(mesh):
    return jax.shard_map(
        program,
        mesh=mesh,
        in_specs=(
            P("tm", None, None, "slab", None, None),
            P("tm", None, "slab", None, None),
            P("slab", None, None),
            P("slab", None, None),
        ),
        out_specs=P("tm", None, None, "slab", None, None),
        check_vma=False,
    )
```

```python
import jax
import jax.numpy as jnp
from jax import lax
from jax.experimental import pallas as pl
from jax.experimental.pallas import tpu as pltpu
from jax.sharding import PartitionSpec as P


AX = ("tm", "slab")
F32 = jnp.float32
W1 = (5.0 / 12.0, 2.0 / 3.0, -1.0 / 12.0)
W2 = (-1.0 / 12.0, 2.0 / 3.0, 5.0 / 12.0)
R1 = (5.0 / 12.0, 2.0 / 3.0 - 1.0, -1.0 / 12.0)
R2 = (-1.0 / 12.0, 2.0 / 3.0, 5.0 / 12.0 - 1.0)
DIFF = (0.1, 0.05)
VM = pl.BlockSpec(memory_space=pltpu.VMEM)
SM = pl.BlockSpec(memory_space=pltpu.SMEM)
SMALL = pltpu.CompilerParams(vmem_limit_bytes=16 * 1024 * 1024)


def flat(z, yh, chip, core):
    return (2 * chip + core) * 32 + (z % 16) * 2 + yh


def everyone():
    return [(z, yh, chip, core) for z in range(16) for yh in range(2)
            for chip in range(8) for core in range(2)]


def pair_groups():
    return [[flat(z, 0, c, k), flat(z, 1, c, k)] for z in range(16) for c in range(8) for k in range(2)]


def core_groups():
    return [[flat(z, h, c, 0), flat(z, h, c, 1)] for z in range(16) for h in range(2) for c in range(8)]


def z_pairs(step):
    return [(flat(z, h, c, k), flat(z + step, h, c, k)) for z, h, c, k in everyone()]


def split_pairs(step):
    return [(flat(z, h, c, k), flat(z + (step if k == 0 else -step), h, c, k))
            for z, h, c, k in everyone()]


def slice_pairs():
    return [(t * 32 + s, (t + 1) * 32 + s) for t in range(15) for s in range(32)]


def turn_pairs(turn):
    return [(flat(z, h, turn, k), flat(z + (2 if k == 0 else -2), h ^ k, turn + 1, k))
            for z in range(16) for h in range(2) for k in range(2)]


def gather(x, groups):
    return lax.all_gather(x, AX, axis=0, axis_index_groups=groups, tiled=False)


def lane(x, n):
    return pltpu.roll(x, n % 128, x.ndim - 1)


def sub(x, n):
    return pltpu.roll(x, n % 8, x.ndim - 2)


def fine_lap(win, coef):
    n = win.shape[0] - 4
    mid = win[2:n + 2]
    near = win[1:n + 1] + win[3:n + 3]
    far = win[0:n] + win[4:n + 4]
    even = mid[:, 0]
    odd = mid[:, 1]
    even_up, even_dn = sub(even, 1), sub(even, -1)
    odd_up, odd_dn = sub(odd, 1), sub(odd, -1)
    nx = jnp.stack([odd + odd_up, even + even_dn], axis=1)
    fx = jnp.stack([even_up + even_dn, odd_up + odd_dn], axis=1)
    near = near + nx + (lane(mid, 1) + lane(mid, -1))
    far = far + fx + (lane(mid, 2) + lane(mid, -2))
    return (coef * 16.0 / 12.0) * near - (coef / 12.0) * far - (coef * 90.0 / 12.0) * mid


def coarse_lap(win, coef):
    n = win.shape[0] - 4
    mid = win[2:n + 2]
    near = win[1:n + 1] + win[3:n + 3] + (sub(mid, 1) + sub(mid, -1))
    far = win[0:n] + win[4:n + 4] + (sub(mid, 2) + sub(mid, -2))
    near_y = lane(mid, 1) + lane(mid, -1)
    far_y = lane(mid, 2) + lane(mid, -2)
    c = coef / 12.0
    return (4.0 * c) * near - (0.25 * c) * far + (16.0 * c) * near_y - c * far_y - (45.0 * c) * mid


def solve(bu, bv, g, ru, rv):
    u = (bu - g) * ru
    v = (bv + g) * rv
    g = u * v * v
    return (bu - g) * ru, (bv + g) * rv


def comb(w, xs):
    return w[0] * xs[0] + w[1] * xs[1] + w[2] * xs[2]


def unrolled(count, step):
    for n in range(count):
        step(n, 0)


def pack_kernel(nv, st, fr, kr, out):
    for p in range(4):
        for par in range(2):
            rows = pl.ds(par, 8, stride=2)
            for j in range(3):
                for s in range(2):
                    out[p, 2 * j + s, par] = nv[0, j, s, p, rows, :]
            for s in range(2):
                out[p, 6 + s, par] = st[0, s, p, rows, :]
            out[p, 8, par] = fr[p, rows, :]
            out[p, 9, par] = kr[p, rows, :]


def first_combo(w, start):
    return start + (5.0 / 12.0 - 1.0) * w[0] + (2.0 / 3.0) * w[1] - (1.0 / 12.0) * w[2]


def sweep_kernel(pair, lo, hi, big, unit, start, rates, v1, v2, b2, xs, xp, cs):
    segs = ((lo, 2, 6), (pair, 8, 8), (hi, 16, 6))

    def raw(ref, i, f):
        if ref is pair:
            return ref[pl.ds(i, 2), f]
        return jnp.stack([ref[i * 10 + f], ref[i * 10 + 10 + f]])

    for s in range(2):
        v1[0, s] = lo[60 + s]
        v1[1, s] = lo[62 + s]
        v1[22, s] = hi[60 + s]
        v1[23, s] = hi[62 + s]

    for ref, base, count in segs:
        def load_v1(n, _, ref=ref, base=base):
            i = 2 * n
            for s in range(2):
                w = [raw(ref, i, 2 * j + s) for j in range(3)]
                start = raw(ref, i, 6 + s)
                v1[pl.ds(base + i, 2), s] = first_combo(w, start)
            return 0

        unrolled(count // 2, load_v1)

    for ref, base, count in segs:
        def node_one(n, _, ref=ref, base=base):
            i = 2 * n
            p = base + i
            q = p - 2
            u = [raw(ref, i, 2 * j) for j in range(3)]
            v = [raw(ref, i, 2 * j + 1) for j in range(3)]
            su, sv = raw(ref, i, 6), raw(ref, i, 7)
            f = raw(ref, i, 8)
            fk = f + raw(ref, i, 9)
            ru = 1.0 / (1.0 + f)
            rv = 1.0 / (1.0 + fk)
            g = [u[j] * v[j] * v[j] for j in range(3)]
            gq = comb(R1, g)
            bu = su + f - f * comb(R1, u) - gq + fine_lap(v1[pl.ds(p - 2, 6), 0], DIFF[0])
            bv = sv + gq - fk * comb(R1, v) + fine_lap(v1[pl.ds(p - 2, 6), 1], DIFF[1])
            nu, nv = solve(bu, bv, g[1], ru, rv)
            at = pl.ds(q, 2)
            big[at, 0] = su
            big[at, 1] = sv
            big[at, 2] = nu
            big[at, 3] = nv
            big[at, 6] = f
            big[at, 7] = fk
            big[at, 8] = ru
            big[at, 9] = rv
            qu, qv = comb(R2, u), comb(R2, v)
            gq = comb(R2, g)
            v2[at, 0] = nu + qu + (u[2] - u[1])
            v2[at, 1] = nv + qv + (v[2] - v[1])
            b2[at, 0] = nu + f - f * qu - gq
            b2[at, 1] = nv + gq - fk * qv
            b2[at, 2] = g[2]
            return 0

        unrolled(count // 2, node_one)

    def node_two(n, _):
        q = 2 + 2 * n
        at = pl.ds(q, 2)
        bu = b2[at, 0] + fine_lap(v2[pl.ds(q - 2, 6), 0], DIFF[0])
        bv = b2[at, 1] + fine_lap(v2[pl.ds(q - 2, 6), 1], DIFF[1])
        nu, nv = solve(bu, bv, b2[at, 2], big[at, 8], big[at, 9])
        big[at, 4] = nu
        big[at, 5] = nv
        return 0

    unrolled(8, node_two)

    def integrals(n, _):
        q = 4 + 2 * n
        at = pl.ds(q, 2)
        u = [big[at, 2 * j] for j in range(3)]
        v = [big[at, 2 * j + 1] for j in range(3)]
        f, fk = big[at, 6], big[at, 7]
        g = [u[j] * v[j] * v[j] for j in range(3)]
        to = pl.ds(2 * n, 2)
        for m, w in enumerate((W1, W2)):
            xu, xv, gx = comb(w, u), comb(w, v), comb(w, g)
            xs[to, 2 * m] = xu
            xs[to, 2 * m + 1] = xv
            xp[to, 2 * m] = f - f * xu - gx
            xp[to, 2 * m + 1] = gx - fk * xv
        return 0

    unrolled(6, integrals)

    def restrict(x):
        return 0.25 * (x[0, 0] + x[0, 1] + x[1, 0] + x[1, 1])

    def coarsen(n, _):
        at = pl.ds(2 * n, 2)
        for f in range(6):
            cs[n, f] = restrict(big[at, f])
        f = restrict(big[at, 6])
        k = restrict(big[at, 7])
        cs[n, 6] = f
        cs[n, 7] = k
        start[n, 0] = cs[n, 0]
        start[n, 1] = cs[n, 1]
        rates[n, 0] = 1.0 / (1.0 + f)
        rates[n, 1] = 1.0 / (1.0 + k)
        return 0

    unrolled(10, coarsen)

    def make_unit(n, _):
        for m in range(2):
            cu, cv = cs[3 + n, 2 * m + 2], cs[3 + n, 2 * m + 3]
            f, fk = cs[3 + n, 6], cs[3 + n, 7]
            g = cu * cv * cv
            for s in range(2):
                fl = fine_lap(xs[pl.ds(2 * n, 6), 2 * m + s], DIFF[s]) + xp[pl.ds(2 * n + 2, 2), 2 * m + s]
                val = restrict(fl) - coarse_lap(cs[pl.ds(n + 1, 5), 2 * m + s], DIFF[s])[0]
                if s == 0:
                    val = val + f * cu + g
                else:
                    val = val - g + fk * cv
                unit[m, n, s] = val
            unit[m, n, 2] = g
        return 0

    unrolled(4, make_unit)


def coarse_node(src, prm, rates, rate_off, dst, count):
    def step(n, _):
        i = 4 * n
        at = pl.ds(i, 4)
        ra = pl.ds(rate_off + i, 4)
        wu = src[pl.ds(i, 8), 0]
        wv = src[pl.ds(i, 8), 1]
        bu = wu[2:6] + coarse_lap(wu, DIFF[0]) + prm[at, 0]
        bv = wv[2:6] + coarse_lap(wv, DIFF[1]) + prm[at, 1]
        nu, nv = solve(bu, bv, prm[at, 2], rates[ra, 0], rates[ra, 1])
        dst[at, 0] = nu
        dst[at, 1] = nv

    unrolled(count // 4, step)


def two_slices(a, prm, n1, n2, n3, out):
    p1a, p2a, p1b, p2b, rates = prm
    coarse_node(a, p1a, rates, 0, n1, 28)
    coarse_node(n1, p2a, rates, 2, n2, 24)
    coarse_node(n2, p1b, rates, 4, n3, 20)
    coarse_node(n3, p2b, rates, 6, out, 16)


def chain_kernel(a, p1a, p2a, p1b, p2b, rates, out, n1, n2, n3):
    two_slices(a, (p1a, p2a, p1b, p2b, rates), n1, n2, n3, out)


def last_kernel(sc, a, p1a, p2a, p1b, p2b, rates, big, prev, res, n1, n2, n3, n4, gs, v1, tp):
    two_slices(a, (p1a, p2a, p1b, p2b, rates), n1, n2, n3, n4)
    core = sc[0]
    yh = sc[1]

    @pl.when(core == 0)
    def _():
        for s in range(2):
            gs[:, s] = a[12:20, s]
            gs[:, 2 + s] = n1[10:18, s]
            gs[:, 4 + s] = n2[8:16, s]

    @pl.when(core != 0)
    def _():
        for s in range(2):
            gs[:, s] = n2[8:16, s]
            gs[:, 2 + s] = n3[6:14, s]
            gs[:, 4 + s] = n4[4:12, s]

    def restrict(x):
        return 0.25 * (x[0, 0] + x[0, 1] + x[1, 0] + x[1, 1])

    def update(i, _):
        row = 2 * yh + i
        at = pl.ds(2 + 4 * yh + 2 * i, 2)
        to = pl.ds(2 * i, 2)
        new = []
        for f in range(6):
            x = big[at, f]
            new.append(x + (gs[row, f] - restrict(x))[None, None])
        u, v = new[0::2], new[1::2]
        bu = prev[to, 0]
        bv = prev[to, 1]
        bu = bu + (gs[row, 0] - restrict(bu))[None, None]
        bv = bv + (gs[row, 1] - restrict(bv))[None, None]
        f, fk = big[at, 6], big[at, 7]
        g = [u[j] * v[j] * v[j] for j in range(3)]
        qu, qv, gq = comb(R1, u), comb(R1, v), comb(R1, g)
        v1[to, 0] = bu + qu + (u[1] - u[0])
        v1[to, 1] = bv + qv + (v[1] - v[0])
        tp[to, 0] = bu + f - f * qu - gq
        tp[to, 1] = bv + gq - fk * qv
        tp[to, 2] = g[1]
        qu, qv, gq = comb(R2, u), comb(R2, v), comb(R2, g)
        tp[to, 3] = qu + (u[2] - u[1])
        tp[to, 4] = qv + (v[2] - v[1])
        tp[to, 5] = f - f * qu - gq
        tp[to, 6] = gq - fk * qv
        tp[to, 7] = g[2]
        tp[to, 8] = bu
        tp[to, 9] = bv
        return 0

    unrolled(6, update)

    def put(node, s, plane, x):
        res[0, node, s, plane, pl.ds(0, 8, stride=2), :] = x[0]
        res[0, node, s, plane, pl.ds(1, 8, stride=2), :] = x[1]

    def node_one(n, _):
        i = 2 + 2 * n
        at = pl.ds(i, 2)
        br = pl.ds(2 + 4 * yh + i, 2)
        bu = tp[at, 0] + fine_lap(v1[pl.ds(i - 2, 6), 0], DIFF[0])
        bv = tp[at, 1] + fine_lap(v1[pl.ds(i - 2, 6), 1], DIFF[1])
        nu, nv = solve(bu, bv, tp[at, 2], big[br, 8], big[br, 9])
        tp[at, 3] = tp[at, 3] + nu
        tp[at, 4] = tp[at, 4] + nv
        tp[at, 5] = tp[at, 5] + nu
        tp[at, 6] = tp[at, 6] + nv
        tp[at, 10] = nu
        tp[at, 11] = nv
        return 0

    unrolled(4, node_one)

    for n in range(2):
        i = 4 + 2 * n
        at = pl.ds(i, 2)
        br = pl.ds(2 + 4 * yh + i, 2)
        bu = tp[at, 5] + fine_lap(tp[pl.ds(i - 2, 6), 3], DIFF[0])
        bv = tp[at, 6] + fine_lap(tp[pl.ds(i - 2, 6), 4], DIFF[1])
        nu, nv = solve(bu, bv, tp[at, 7], big[br, 8], big[br, 9])
        for d in range(2):
            p = 2 * n + d
            put(2, 0, p, nu[d])
            put(2, 1, p, nv[d])
            for s in range(2):
                put(0, s, p, tp[i + d, 8 + s])
                put(1, s, p, tp[i + d, 10 + s])


def vmem(*shape):
    return pltpu.VMEM(shape, F32)


def shape(*dims):
    return jax.ShapeDtypeStruct(dims, F32)


def program(node_values, start_state, feed_rate, kill_rate):
    t = lax.axis_index("tm")
    core = t % 2
    chip = t // 2
    yh = lax.axis_index("slab") % 2
    left = core == 0
    own = pl.pallas_call(
        pack_kernel, out_shape=shape(4, 10, 2, 8, 128), in_specs=[VM] * 4, out_specs=VM,
        name="pack",
    )(node_values, start_state, feed_rate, kill_rate)
    pair = gather(own, pair_groups()).reshape(8, 10, 2, 8, 128)

    def edge(planes, far):
        w = [far[:, 2 * j:2 * j + 2] for j in range(3)]
        v = first_combo(w, far[:, 6:8])
        return jnp.concatenate([planes.reshape(60, 2, 8, 128), v.reshape(4, 2, 8, 128)])

    lo = lax.ppermute(edge(pair[2:8], pair[0:2]), AX, z_pairs(1))
    hi = lax.ppermute(edge(pair[0:6], pair[6:8]), AX, z_pairs(-1))
    big, unit, start, rates = pl.pallas_call(
        sweep_kernel,
        out_shape=(shape(20, 10, 2, 8, 128), shape(2, 4, 3, 8, 128), shape(10, 2, 8, 128),
                   shape(10, 2, 8, 128)),
        in_specs=[VM] * 3, out_specs=(VM, VM, VM, VM),
        scratch_shapes=[vmem(24, 2, 2, 8, 128), vmem(20, 2, 2, 8, 128), vmem(20, 3, 2, 8, 128),
                        vmem(12, 4, 2, 8, 128), vmem(12, 4, 2, 8, 128), vmem(10, 8, 8, 128)],
        name="sweep", compiler_params=SMALL,
    )(pair, lo, hi)

    def rows(parts):
        return jnp.concatenate([x.reshape(-1, 8, 128) for x in parts])

    both = gather(rows([unit, start]), core_groups())
    units = both[:, :24].reshape(2, 2, 4, 3, 8, 128)
    start = both[0, 24:].reshape(10, 2, 8, 128)
    (p1a, p2a), (p1b, p2b) = units

    def near_planes(x, n):
        return jnp.where(left, x[4 - n:], x[:n])

    def send(parts, step):
        message = rows(parts)
        return lax.ppermute(message, AX, split_pairs(step))

    start4 = jnp.where(left, start[0:4], start[6:10])
    rates4 = jnp.where(left, rates[0:4], rates[6:10])
    near = send([p1a, p2a, p1b, p2b, start4, rates4], 1)
    mid = send([p1a, p2a, p1b, near_planes(p2b, 2), start4, rates4], 2)
    far = send([p1a, near_planes(p2a, 2), jnp.where(left, start[1:4], start[6:9]),
                jnp.where(left, rates[3:4], rates[6:7])], 3)
    nears = gather(near, core_groups())
    fars = gather(jnp.concatenate([mid, far]), core_groups())

    def pick(part, side, first, planes, fields):
        return part[side, first:first + planes * fields].reshape(planes, fields, 8, 128)

    def window(own, *pieces):
        below = [pick(part, 0, first, planes, own.shape[1]) for part, first, planes in pieces]
        above = [pick(part, 1, first, planes, own.shape[1]) for part, first, planes in pieces]
        return jnp.concatenate(below[::-1] + [own] + above)

    p1a = window(p1a, (nears, 0, 4), (fars, 0, 4), (fars, 58, 4))
    p2a = window(p2a, (nears, 12, 4), (fars, 12, 4), (fars, 70, 2))
    p1b = window(p1b, (nears, 24, 4), (fars, 24, 4))
    p2b = window(p2b, (nears, 36, 4), (fars, 36, 2))
    state = window(start, (nears, 48, 4), (fars, 42, 4), (fars, 76, 3))
    rates = window(rates, (nears, 56, 4), (fars, 50, 4), (fars, 82, 1))
    prm = (p1a, p2a, p1b, p2b, rates)

    mine = lax.dynamic_slice_in_dim(big, 2 + 4 * yh, 12, 0)
    prev = lax.ppermute(mine[:, 4:6], AX, slice_pairs())
    prev = jnp.where(t == 0, mine[:, 0:2], prev)

    scratch = [vmem(28, 2, 8, 128), vmem(24, 2, 8, 128), vmem(20, 2, 8, 128)]

    for turn in range(7):
        out = pl.pallas_call(
            chain_kernel, out_shape=shape(16, 2, 8, 128), in_specs=[VM] * 6, out_specs=VM,
            scratch_shapes=scratch, name="chain", compiler_params=SMALL,
        )(state, *prm)
        moved = lax.ppermute(out, AX, turn_pairs(turn))
        moved = gather(moved, core_groups()).reshape(32, 2, 8, 128)
        state = jnp.where(chip == turn + 1, moved, state)

    scalars = jnp.stack([core, yh]).astype(jnp.int32)
    return pl.pallas_call(
        last_kernel, out_shape=shape(1, 3, 2, 4, 16, 128), in_specs=[SM] + [VM] * 8, out_specs=VM,
        scratch_shapes=scratch + [
            vmem(16, 2, 8, 128), vmem(8, 6, 8, 128), vmem(12, 2, 2, 8, 128), vmem(12, 12, 2, 8, 128)],
        name="last", compiler_params=SMALL,
    )(scalars, state, *prm, big, prev)


def solution(mesh):
    return jax.shard_map(
        program,
        mesh=mesh,
        in_specs=(
            P("tm", None, None, "slab", None, None),
            P("tm", None, "slab", None, None),
            P("slab", None, None),
            P("slab", None, None),
        ),
        out_specs=P("tm", None, None, "slab", None, None),
        check_vma=False,
    )
```

```python
import jax
import jax.numpy as jnp
from jax import lax
from jax.experimental import pallas as pl
from jax.experimental.pallas import tpu as pltpu
from jax.sharding import PartitionSpec as P


AX = ("tm", "slab")
F32 = jnp.float32
W1 = (5.0 / 12.0, 2.0 / 3.0, -1.0 / 12.0)
W2 = (-1.0 / 12.0, 2.0 / 3.0, 5.0 / 12.0)
R1 = (5.0 / 12.0, 2.0 / 3.0 - 1.0, -1.0 / 12.0)
R2 = (-1.0 / 12.0, 2.0 / 3.0, 5.0 / 12.0 - 1.0)
DIFF = (0.1, 0.05)
VM = pl.BlockSpec(memory_space=pltpu.VMEM)
SM = pl.BlockSpec(memory_space=pltpu.SMEM)
SMALL = pltpu.CompilerParams(vmem_limit_bytes=16 * 1024 * 1024)


def flat(z, yh, chip, core):
    return (2 * chip + core) * 32 + (z % 16) * 2 + yh


def everyone():
    return [(z, yh, chip, core) for z in range(16) for yh in range(2)
            for chip in range(8) for core in range(2)]


def pair_groups():
    return [[flat(z, 0, c, k), flat(z, 1, c, k)] for z in range(16) for c in range(8) for k in range(2)]


def core_groups():
    return [[flat(z, h, c, 0), flat(z, h, c, 1)] for z in range(16) for h in range(2) for c in range(8)]


def z_pairs(step):
    return [(flat(z, h, c, k), flat(z + step, h, c, k)) for z, h, c, k in everyone()]


def split_pairs(step):
    return [(flat(z, h, c, k), flat(z + (step if k == 0 else -step), h, c, k))
            for z, h, c, k in everyone()]


def slice_pairs():
    return [(t * 32 + s, (t + 1) * 32 + s) for t in range(15) for s in range(32)]


def turn_pairs(turn, parity):
    return [(flat(z, h, turn, k), flat(z + (2 if k == 0 else -2), h ^ k, turn + 1, k))
            for z in range(parity, 16, 2) for h in range(2) for k in range(2)]


def edge_pairs():
    return [(flat(z, h, c, k), flat(z + (1 if h == 0 else -1), h, c, k)) for z, h, c, k in everyone()]


def gather(x, groups):
    return lax.all_gather(x, AX, axis=0, axis_index_groups=groups, tiled=False)


def lane(x, n):
    return pltpu.roll(x, n % 128, x.ndim - 1)


def sub(x, n):
    return pltpu.roll(x, n % 8, x.ndim - 2)


def fine_lap(win, coef):
    n = win.shape[0] - 4
    mid = win[2:n + 2]
    near = win[1:n + 1] + win[3:n + 3]
    far = win[0:n] + win[4:n + 4]
    even = mid[:, 0]
    odd = mid[:, 1]
    even_up, even_dn = sub(even, 1), sub(even, -1)
    odd_up, odd_dn = sub(odd, 1), sub(odd, -1)
    nx = jnp.stack([odd + odd_up, even + even_dn], axis=1)
    fx = jnp.stack([even_up + even_dn, odd_up + odd_dn], axis=1)
    near = near + nx + (lane(mid, 1) + lane(mid, -1))
    far = far + fx + (lane(mid, 2) + lane(mid, -2))
    return (coef * 16.0 / 12.0) * near - (coef / 12.0) * far - (coef * 90.0 / 12.0) * mid


def coarse_lap(win, coef):
    n = win.shape[0] - 4
    mid = win[2:n + 2]
    near = win[1:n + 1] + win[3:n + 3] + (sub(mid, 1) + sub(mid, -1))
    far = win[0:n] + win[4:n + 4] + (sub(mid, 2) + sub(mid, -2))
    near_y = lane(mid, 1) + lane(mid, -1)
    far_y = lane(mid, 2) + lane(mid, -2)
    c = coef / 12.0
    return (4.0 * c) * near - (0.25 * c) * far + (16.0 * c) * near_y - c * far_y - (45.0 * c) * mid


def solve(bu, bv, g, ru, rv):
    u = (bu - g) * ru
    v = (bv + g) * rv
    g = u * v * v
    return (bu - g) * ru, (bv + g) * rv


def comb(w, xs):
    return w[0] * xs[0] + w[1] * xs[1] + w[2] * xs[2]


def unrolled(count, step):
    for n in range(count):
        step(n, 0)


def pack_kernel(nv, st, fr, kr, out):
    for p in range(4):
        for par in range(2):
            rows = pl.ds(par, 8, stride=2)
            for j in range(3):
                for s in range(2):
                    out[p, 2 * j + s, par] = nv[0, j, s, p, rows, :]
            for s in range(2):
                out[p, 6 + s, par] = st[0, s, p, rows, :]
            out[p, 8, par] = fr[p, rows, :]
            out[p, 9, par] = kr[p, rows, :]


def first_combo(w, start):
    return start + (5.0 / 12.0 - 1.0) * w[0] + (2.0 / 3.0) * w[1] - (1.0 / 12.0) * w[2]


def sweep_kernel(pair, lo, hi, big, unit, start, rates, v1, v2, b2, xs, xp, cs):
    segs = ((lo, 2, 4), (pair, 6, 8), (hi, 14, 4))

    def raw(ref, i, f):
        if ref is pair:
            return ref[pl.ds(i, 2), f]
        return jnp.stack([ref[i * 10 + f], ref[i * 10 + 10 + f]])

    for s in range(2):
        v1[0, s] = lo[40 + s]
        v1[1, s] = lo[42 + s]
        v1[18, s] = hi[40 + s]
        v1[19, s] = hi[42 + s]

    for ref, base, count in segs:
        def load_v1(n, _, ref=ref, base=base):
            i = 2 * n
            for s in range(2):
                w = [raw(ref, i, 2 * j + s) for j in range(3)]
                start = raw(ref, i, 6 + s)
                v1[pl.ds(base + i, 2), s] = first_combo(w, start)
            return 0

        unrolled(count // 2, load_v1)

    for ref, base, count in segs:
        def node_one(n, _, ref=ref, base=base):
            i = 2 * n
            p = base + i
            q = p - 2
            u = [raw(ref, i, 2 * j) for j in range(3)]
            v = [raw(ref, i, 2 * j + 1) for j in range(3)]
            su, sv = raw(ref, i, 6), raw(ref, i, 7)
            f = raw(ref, i, 8)
            fk = f + raw(ref, i, 9)
            ru = 1.0 / (1.0 + f)
            rv = 1.0 / (1.0 + fk)
            g = [u[j] * v[j] * v[j] for j in range(3)]
            gq = comb(R1, g)
            bu = su + f - f * comb(R1, u) - gq + fine_lap(v1[pl.ds(p - 2, 6), 0], DIFF[0])
            bv = sv + gq - fk * comb(R1, v) + fine_lap(v1[pl.ds(p - 2, 6), 1], DIFF[1])
            nu, nv = solve(bu, bv, g[1], ru, rv)
            at = pl.ds(q, 2)
            big[at, 0] = su
            big[at, 1] = sv
            big[at, 2] = nu
            big[at, 3] = nv
            big[at, 6] = f
            big[at, 7] = fk
            big[at, 8] = ru
            big[at, 9] = rv
            qu, qv = comb(R2, u), comb(R2, v)
            gq = comb(R2, g)
            v2[at, 0] = nu + qu + (u[2] - u[1])
            v2[at, 1] = nv + qv + (v[2] - v[1])
            b2[at, 0] = nu + f - f * qu - gq
            b2[at, 1] = nv + gq - fk * qv
            b2[at, 2] = g[2]
            return 0

        unrolled(count // 2, node_one)

    def node_two(n, _):
        q = 2 + 2 * n
        at = pl.ds(q, 2)
        bu = b2[at, 0] + fine_lap(v2[pl.ds(q - 2, 6), 0], DIFF[0])
        bv = b2[at, 1] + fine_lap(v2[pl.ds(q - 2, 6), 1], DIFF[1])
        nu, nv = solve(bu, bv, b2[at, 2], big[at, 8], big[at, 9])
        big[at, 4] = nu
        big[at, 5] = nv
        return 0

    unrolled(6, node_two)

    def integrals(n, _):
        q = 2 + 2 * n
        at = pl.ds(q, 2)
        u = [big[at, 2 * j] for j in range(3)]
        v = [big[at, 2 * j + 1] for j in range(3)]
        f, fk = big[at, 6], big[at, 7]
        g = [u[j] * v[j] * v[j] for j in range(3)]
        to = pl.ds(2 * n, 2)
        for m, w in enumerate((W1, W2)):
            xu, xv, gx = comb(w, u), comb(w, v), comb(w, g)
            xs[to, 2 * m] = xu
            xs[to, 2 * m + 1] = xv
            xp[to, 2 * m] = f - f * xu - gx
            xp[to, 2 * m + 1] = gx - fk * xv
        return 0

    unrolled(6, integrals)

    def restrict(x):
        return 0.25 * (x[0, 0] + x[0, 1] + x[1, 0] + x[1, 1])

    def coarsen(n, _):
        at = pl.ds(2 * n, 2)
        for f in range(6 if 1 <= n <= 6 else 4):
            cs[n, f] = restrict(big[at, f])
        f = restrict(big[at, 6])
        k = restrict(big[at, 7])
        cs[n, 6] = f
        cs[n, 7] = k
        start[n, 0] = cs[n, 0]
        start[n, 1] = cs[n, 1]
        rates[n, 0] = 1.0 / (1.0 + f)
        rates[n, 1] = 1.0 / (1.0 + k)
        return 0

    unrolled(8, coarsen)

    def make_unit(n, _):
        for m in range(2):
            cu, cv = cs[2 + n, 2 * m + 2], cs[2 + n, 2 * m + 3]
            f, fk = cs[2 + n, 6], cs[2 + n, 7]
            g = cu * cv * cv
            for s in range(2):
                fl = fine_lap(xs[pl.ds(2 * n, 6), 2 * m + s], DIFF[s]) + xp[pl.ds(2 * n + 2, 2), 2 * m + s]
                val = restrict(fl) - coarse_lap(cs[pl.ds(n, 5), 2 * m + s], DIFF[s])[0]
                if s == 0:
                    val = val + f * cu + g
                else:
                    val = val - g + fk * cv
                unit[m, n, s] = val
            unit[m, n, 2] = g
        return 0

    unrolled(4, make_unit)


def coarse_node(src, prm, rates, rate_off, dst, count):
    def step(n, _):
        i = 4 * n
        at = pl.ds(i, 4)
        ra = pl.ds(rate_off + i, 4)
        wu = src[pl.ds(i, 8), 0]
        wv = src[pl.ds(i, 8), 1]
        bu = wu[2:6] + coarse_lap(wu, DIFF[0]) + prm[at, 0]
        bv = wv[2:6] + coarse_lap(wv, DIFF[1]) + prm[at, 1]
        nu, nv = solve(bu, bv, prm[at, 2], rates[ra, 0], rates[ra, 1])
        dst[at, 0] = nu
        dst[at, 1] = nv

    unrolled(count // 4, step)


def two_slices(a, prm, n1, n2, n3, out):
    p1a, p2a, p1b, p2b, rates = prm
    coarse_node(a, p1a, rates, 0, n1, 28)
    coarse_node(n1, p2a, rates, 2, n2, 24)
    coarse_node(n2, p1b, rates, 4, n3, 20)
    coarse_node(n3, p2b, rates, 6, out, 16)


def chain_kernel(a, p1a, p2a, p1b, p2b, rates, out, n1, n2, n3):
    two_slices(a, (p1a, p2a, p1b, p2b, rates), n1, n2, n3, out)


def last_kernel(sc, a, p1a, p2a, p1b, p2b, rates, big, end, prev, res, n1, n2, n3, n4, gs, v1, tp):
    two_slices(a, (p1a, p2a, p1b, p2b, rates), n1, n2, n3, n4)
    core = sc[0]
    yh = sc[1]

    @pl.when(core == 0)
    def _():
        for s in range(2):
            gs[:, s] = a[12:20, s]
            gs[:, 2 + s] = n1[10:18, s]
            gs[:, 4 + s] = n2[8:16, s]

    @pl.when(core != 0)
    def _():
        for s in range(2):
            gs[:, s] = n2[8:16, s]
            gs[:, 2 + s] = n3[6:14, s]
            gs[:, 4 + s] = n4[4:12, s]

    def restrict(x):
        return 0.25 * (x[0, 0] + x[0, 1] + x[1, 0] + x[1, 1])

    def update(i, _):
        row = 2 * yh + i
        at = pl.ds(4 * yh + 2 * i, 2)
        to = pl.ds(2 * i, 2)
        new = []
        for f in range(6):
            x = big[at, f] if f < 4 else end[to, f - 4]
            new.append(x + (gs[row, f] - restrict(x))[None, None])
        u, v = new[0::2], new[1::2]
        bu = prev[to, 0]
        bv = prev[to, 1]
        bu = bu + (gs[row, 0] - restrict(bu))[None, None]
        bv = bv + (gs[row, 1] - restrict(bv))[None, None]
        f, fk = big[at, 6], big[at, 7]
        g = [u[j] * v[j] * v[j] for j in range(3)]
        qu, qv, gq = comb(R1, u), comb(R1, v), comb(R1, g)
        v1[to, 0] = bu + qu + (u[1] - u[0])
        v1[to, 1] = bv + qv + (v[1] - v[0])
        tp[to, 0] = bu + f - f * qu - gq
        tp[to, 1] = bv + gq - fk * qv
        tp[to, 2] = g[1]
        qu, qv, gq = comb(R2, u), comb(R2, v), comb(R2, g)
        tp[to, 3] = qu + (u[2] - u[1])
        tp[to, 4] = qv + (v[2] - v[1])
        tp[to, 5] = f - f * qu - gq
        tp[to, 6] = gq - fk * qv
        tp[to, 7] = g[2]
        tp[to, 8] = bu
        tp[to, 9] = bv
        return 0

    unrolled(6, update)

    def put(node, s, plane, x):
        res[0, node, s, plane, pl.ds(0, 8, stride=2), :] = x[0]
        res[0, node, s, plane, pl.ds(1, 8, stride=2), :] = x[1]

    def node_one(n, _):
        i = 2 + 2 * n
        at = pl.ds(i, 2)
        br = pl.ds(4 * yh + i, 2)
        bu = tp[at, 0] + fine_lap(v1[pl.ds(i - 2, 6), 0], DIFF[0])
        bv = tp[at, 1] + fine_lap(v1[pl.ds(i - 2, 6), 1], DIFF[1])
        nu, nv = solve(bu, bv, tp[at, 2], big[br, 8], big[br, 9])
        tp[at, 3] = tp[at, 3] + nu
        tp[at, 4] = tp[at, 4] + nv
        tp[at, 5] = tp[at, 5] + nu
        tp[at, 6] = tp[at, 6] + nv
        tp[at, 10] = nu
        tp[at, 11] = nv
        return 0

    unrolled(4, node_one)

    for n in range(2):
        i = 4 + 2 * n
        at = pl.ds(i, 2)
        br = pl.ds(4 * yh + i, 2)
        bu = tp[at, 5] + fine_lap(tp[pl.ds(i - 2, 6), 3], DIFF[0])
        bv = tp[at, 6] + fine_lap(tp[pl.ds(i - 2, 6), 4], DIFF[1])
        nu, nv = solve(bu, bv, tp[at, 7], big[br, 8], big[br, 9])
        for d in range(2):
            p = 2 * n + d
            put(2, 0, p, nu[d])
            put(2, 1, p, nv[d])
            for s in range(2):
                put(0, s, p, tp[i + d, 8 + s])
                put(1, s, p, tp[i + d, 10 + s])


def vmem(*shape):
    return pltpu.VMEM(shape, F32)


def shape(*dims):
    return jax.ShapeDtypeStruct(dims, F32)


def program(node_values, start_state, feed_rate, kill_rate):
    t = lax.axis_index("tm")
    core = t % 2
    chip = t // 2
    yh = lax.axis_index("slab") % 2
    left = core == 0
    even_z = (lax.axis_index("slab") // 2) % 2 == 0
    own = pl.pallas_call(
        pack_kernel, out_shape=shape(4, 10, 2, 8, 128), in_specs=[VM] * 4, out_specs=VM,
        name="pack",
    )(node_values, start_state, feed_rate, kill_rate)
    pair = gather(own, pair_groups()).reshape(8, 10, 2, 8, 128)

    def edge(planes, far):
        w = [far[:, 2 * j:2 * j + 2] for j in range(3)]
        v = first_combo(w, far[:, 6:8])
        return jnp.concatenate([planes.reshape(40, 2, 8, 128), v.reshape(4, 2, 8, 128)])

    lo = lax.ppermute(edge(pair[4:8], pair[2:4]), AX, z_pairs(1))
    hi = lax.ppermute(edge(pair[0:4], pair[4:6]), AX, z_pairs(-1))
    big, unit, start, rates = pl.pallas_call(
        sweep_kernel,
        out_shape=(shape(16, 10, 2, 8, 128), shape(2, 4, 3, 8, 128), shape(8, 2, 8, 128),
                   shape(8, 2, 8, 128)),
        in_specs=[VM] * 3, out_specs=(VM, VM, VM, VM),
        scratch_shapes=[vmem(20, 2, 2, 8, 128), vmem(16, 2, 2, 8, 128), vmem(16, 3, 2, 8, 128),
                        vmem(12, 4, 2, 8, 128), vmem(12, 4, 2, 8, 128), vmem(8, 8, 8, 128)],
        name="sweep", compiler_params=SMALL,
    )(pair, lo, hi)

    def rows(parts):
        return jnp.concatenate([x.reshape(-1, 8, 128) for x in parts])

    both = gather(rows([unit, start]), core_groups())
    units = both[:, :24].reshape(2, 2, 4, 3, 8, 128)
    start = both[0, 24:].reshape(8, 2, 8, 128)
    (p1a, p2a), (p1b, p2b) = units

    def near_planes(x, n):
        return jnp.where(left, x[4 - n:], x[:n])

    def send(parts, step):
        message = rows(parts)
        return lax.ppermute(message, AX, split_pairs(step))

    start4 = jnp.where(left, start[0:4], start[4:8])
    rates4 = jnp.where(left, rates[0:4], rates[4:8])
    near = send([p1a, p2a, p1b, p2b, start4, rates4], 1)
    mid = send([p1a, p2a, p1b, near_planes(p2b, 2), start4, rates4], 2)
    far = send([p1a, near_planes(p2a, 2), start4, jnp.where(left, rates[2:4], rates[4:6])], 3)
    nears = gather(near, core_groups())
    fars = gather(jnp.concatenate([mid, far]), core_groups())

    def pick(part, side, first, planes, fields):
        return part[side, first:first + planes * fields].reshape(planes, fields, 8, 128)

    def window(own, *pieces):
        below = [pick(part, 0, first, planes, own.shape[1]) for part, first, planes in pieces]
        above = [pick(part, 1, first, planes, own.shape[1]) for part, first, planes in pieces]
        return jnp.concatenate(below[::-1] + [own] + above)

    p1a = window(p1a, (nears, 0, 4), (fars, 0, 4), (fars, 58, 4))
    p2a = window(p2a, (nears, 12, 4), (fars, 12, 4), (fars, 70, 2))
    p1b = window(p1b, (nears, 24, 4), (fars, 24, 4))
    p2b = window(p2b, (nears, 36, 4), (fars, 36, 2))
    state = window(start, (nears, 48, 4), (fars, 42, 4), (fars, 76, 4))
    rates = window(rates, (nears, 56, 4), (fars, 50, 4), (fars, 84, 2))
    prm = (p1a, p2a, p1b, p2b, rates)

    lower = yh == 0
    outer = lax.ppermute(jnp.where(lower, big[8:10, 4:6], big[6:8, 4:6]), AX, edge_pairs())
    end = jnp.where(lower, jnp.concatenate([outer, big[2:12, 4:6]]),
                    jnp.concatenate([big[4:14, 4:6], outer]))
    prev = lax.ppermute(end, AX, slice_pairs())
    prev = jnp.where(t == 0, jnp.where(lower, big[0:12, 0:2], big[4:16, 0:2]), prev)

    scratch = [vmem(28, 2, 8, 128), vmem(24, 2, 8, 128), vmem(20, 2, 8, 128)]

    for turn in range(7):
        out = pl.pallas_call(
            chain_kernel, out_shape=shape(16, 2, 8, 128), in_specs=[VM] * 6, out_specs=VM,
            scratch_shapes=scratch, name="chain", compiler_params=SMALL,
        )(state, *prm)
        even = lax.ppermute(out, AX, turn_pairs(turn, 0))
        odd = lax.ppermute(out, AX, turn_pairs(turn, 1))
        moved = jnp.where(even_z, even, odd)
        moved = gather(moved, core_groups()).reshape(32, 2, 8, 128)
        state = jnp.where(chip == turn + 1, moved, state)

    scalars = jnp.stack([core, yh]).astype(jnp.int32)
    return pl.pallas_call(
        last_kernel, out_shape=shape(1, 3, 2, 4, 16, 128), in_specs=[SM] + [VM] * 9, out_specs=VM,
        scratch_shapes=scratch + [
            vmem(16, 2, 8, 128), vmem(8, 6, 8, 128), vmem(12, 2, 2, 8, 128), vmem(12, 12, 2, 8, 128)],
        name="last", compiler_params=SMALL,
    )(scalars, state, *prm, big, end, prev)


def solution(mesh):
    return jax.shard_map(
        program,
        mesh=mesh,
        in_specs=(
            P("tm", None, None, "slab", None, None),
            P("tm", None, "slab", None, None),
            P("slab", None, None),
            P("slab", None, None),
        ),
        out_specs=P("tm", None, None, "slab", None, None),
        check_vma=False,
    )
```

```python
import jax
import jax.numpy as jnp
from jax import lax
from jax.experimental import pallas as pl
from jax.experimental.pallas import tpu as pltpu
from jax.sharding import PartitionSpec as P


AX = ("tm", "slab")
F32 = jnp.float32
W1 = (5.0 / 12.0, 2.0 / 3.0, -1.0 / 12.0)
W2 = (-1.0 / 12.0, 2.0 / 3.0, 5.0 / 12.0)
R1 = (5.0 / 12.0, 2.0 / 3.0 - 1.0, -1.0 / 12.0)
R2 = (-1.0 / 12.0, 2.0 / 3.0, 5.0 / 12.0 - 1.0)
DIFF = (0.1, 0.05)
VM = pl.BlockSpec(memory_space=pltpu.VMEM)
SM = pl.BlockSpec(memory_space=pltpu.SMEM)
SMALL = pltpu.CompilerParams(vmem_limit_bytes=16 * 1024 * 1024)


def flat(z, yh, chip, core):
    return (2 * chip + core) * 32 + (z % 16) * 2 + yh


def everyone():
    return [(z, yh, chip, core) for z in range(16) for yh in range(2)
            for chip in range(8) for core in range(2)]


def pair_groups():
    return [[flat(z, 0, c, k), flat(z, 1, c, k)] for z in range(16) for c in range(8) for k in range(2)]


def core_groups():
    return [[flat(z, h, c, 0), flat(z, h, c, 1)] for z in range(16) for h in range(2) for c in range(8)]


def z_pairs(step):
    return [(flat(z, h, c, k), flat(z + step, h, c, k)) for z, h, c, k in everyone()]


def split_pairs(step):
    return [(flat(z, h, c, k), flat(z + (step if k == 0 else -step), h, c, k))
            for z, h, c, k in everyone()]


def slice_pairs():
    return [(t * 32 + s, (t + 1) * 32 + s) for t in range(15) for s in range(32)]


def turn_pairs(turn):
    return [(flat(z, h, turn, k), flat(z + (2 if k == 0 else -2), h ^ k, turn + 1, k))
            for z in range(16) for h in range(2) for k in range(2)]


def edge_pairs():
    return [(flat(z, h, c, k), flat(z + (1 if h == 0 else -1), h, c, k)) for z, h, c, k in everyone()]


def gather(x, groups):
    return lax.all_gather(x, AX, axis=0, axis_index_groups=groups, tiled=False)


def lane(x, n):
    return pltpu.roll(x, n % 128, x.ndim - 1)


def sub(x, n):
    return pltpu.roll(x, n % 8, x.ndim - 2)


def fine_lap(win, coef):
    n = win.shape[0] - 4
    mid = win[2:n + 2]
    near = win[1:n + 1] + win[3:n + 3]
    far = win[0:n] + win[4:n + 4]
    even = mid[:, 0]
    odd = mid[:, 1]
    even_up, even_dn = sub(even, 1), sub(even, -1)
    odd_up, odd_dn = sub(odd, 1), sub(odd, -1)
    nx = jnp.stack([odd + odd_up, even + even_dn], axis=1)
    fx = jnp.stack([even_up + even_dn, odd_up + odd_dn], axis=1)
    near = near + nx + (lane(mid, 1) + lane(mid, -1))
    far = far + fx + (lane(mid, 2) + lane(mid, -2))
    return (coef * 16.0 / 12.0) * near - (coef / 12.0) * far - (coef * 90.0 / 12.0) * mid


def coarse_lap(win, coef):
    n = win.shape[0] - 4
    mid = win[2:n + 2]
    near = win[1:n + 1] + win[3:n + 3] + (sub(mid, 1) + sub(mid, -1))
    far = win[0:n] + win[4:n + 4] + (sub(mid, 2) + sub(mid, -2))
    near_y = lane(mid, 1) + lane(mid, -1)
    far_y = lane(mid, 2) + lane(mid, -2)
    c = coef / 12.0
    return (4.0 * c) * near - (0.25 * c) * far + (16.0 * c) * near_y - c * far_y - (45.0 * c) * mid


def solve(bu, bv, g, ru, rv):
    u = (bu - g) * ru
    v = (bv + g) * rv
    g = u * v * v
    return (bu - g) * ru, (bv + g) * rv


def comb(w, xs):
    return w[0] * xs[0] + w[1] * xs[1] + w[2] * xs[2]


def unrolled(count, step):
    for n in range(count):
        step(n, 0)


def pack_kernel(nv, st, fr, kr, out):
    for p in range(4):
        for par in range(2):
            rows = pl.ds(par, 8, stride=2)
            for j in range(3):
                for s in range(2):
                    out[p, 2 * j + s, par] = nv[0, j, s, p, rows, :]
            for s in range(2):
                out[p, 6 + s, par] = st[0, s, p, rows, :]
            out[p, 8, par] = fr[p, rows, :]
            out[p, 9, par] = kr[p, rows, :]


def first_combo(w, start):
    return start + (5.0 / 12.0 - 1.0) * w[0] + (2.0 / 3.0) * w[1] - (1.0 / 12.0) * w[2]


def sweep_kernel(pair, lo, hi, big, unit, start, rates, v1, v2, b2, xs, xp, cs):
    segs = ((lo, 2, 4), (pair, 6, 8), (hi, 14, 4))

    def raw(ref, i, f):
        if ref is pair:
            return ref[pl.ds(i, 2), f]
        return jnp.stack([ref[i * 10 + f], ref[i * 10 + 10 + f]])

    for s in range(2):
        v1[0, s] = lo[40 + s]
        v1[1, s] = lo[42 + s]
        v1[18, s] = hi[40 + s]
        v1[19, s] = hi[42 + s]

    for ref, base, count in segs:
        def load_v1(n, _, ref=ref, base=base):
            i = 2 * n
            for s in range(2):
                w = [raw(ref, i, 2 * j + s) for j in range(3)]
                start = raw(ref, i, 6 + s)
                v1[pl.ds(base + i, 2), s] = first_combo(w, start)
            return 0

        unrolled(count // 2, load_v1)

    for ref, base, count in segs:
        def node_one(n, _, ref=ref, base=base):
            i = 2 * n
            p = base + i
            q = p - 2
            u = [raw(ref, i, 2 * j) for j in range(3)]
            v = [raw(ref, i, 2 * j + 1) for j in range(3)]
            su, sv = raw(ref, i, 6), raw(ref, i, 7)
            f = raw(ref, i, 8)
            fk = f + raw(ref, i, 9)
            ru = 1.0 / (1.0 + f)
            rv = 1.0 / (1.0 + fk)
            g = [u[j] * v[j] * v[j] for j in range(3)]
            gq = comb(R1, g)
            bu = su + f - f * comb(R1, u) - gq + fine_lap(v1[pl.ds(p - 2, 6), 0], DIFF[0])
            bv = sv + gq - fk * comb(R1, v) + fine_lap(v1[pl.ds(p - 2, 6), 1], DIFF[1])
            nu, nv = solve(bu, bv, g[1], ru, rv)
            at = pl.ds(q, 2)
            big[at, 0] = su
            big[at, 1] = sv
            big[at, 2] = nu
            big[at, 3] = nv
            big[at, 6] = f
            big[at, 7] = fk
            big[at, 8] = ru
            big[at, 9] = rv
            qu, qv = comb(R2, u), comb(R2, v)
            gq = comb(R2, g)
            v2[at, 0] = nu + qu + (u[2] - u[1])
            v2[at, 1] = nv + qv + (v[2] - v[1])
            b2[at, 0] = nu + f - f * qu - gq
            b2[at, 1] = nv + gq - fk * qv
            b2[at, 2] = g[2]
            return 0

        unrolled(count // 2, node_one)

    def node_two(n, _):
        q = 2 + 2 * n
        at = pl.ds(q, 2)
        bu = b2[at, 0] + fine_lap(v2[pl.ds(q - 2, 6), 0], DIFF[0])
        bv = b2[at, 1] + fine_lap(v2[pl.ds(q - 2, 6), 1], DIFF[1])
        nu, nv = solve(bu, bv, b2[at, 2], big[at, 8], big[at, 9])
        big[at, 4] = nu
        big[at, 5] = nv
        return 0

    unrolled(6, node_two)

    def integrals(n, _):
        q = 2 + 2 * n
        at = pl.ds(q, 2)
        u = [big[at, 2 * j] for j in range(3)]
        v = [big[at, 2 * j + 1] for j in range(3)]
        f, fk = big[at, 6], big[at, 7]
        g = [u[j] * v[j] * v[j] for j in range(3)]
        to = pl.ds(2 * n, 2)
        for m, w in enumerate((W1, W2)):
            xu, xv, gx = comb(w, u), comb(w, v), comb(w, g)
            xs[to, 2 * m] = xu
            xs[to, 2 * m + 1] = xv
            xp[to, 2 * m] = f - f * xu - gx
            xp[to, 2 * m + 1] = gx - fk * xv
        return 0

    unrolled(6, integrals)

    def restrict(x):
        return 0.25 * (x[0, 0] + x[0, 1] + x[1, 0] + x[1, 1])

    def coarsen(n, _):
        at = pl.ds(2 * n, 2)
        for f in range(6 if 1 <= n <= 6 else 4):
            cs[n, f] = restrict(big[at, f])
        f = restrict(big[at, 6])
        k = restrict(big[at, 7])
        cs[n, 6] = f
        cs[n, 7] = k
        start[n, 0] = cs[n, 0]
        start[n, 1] = cs[n, 1]
        rates[n, 0] = 1.0 / (1.0 + f)
        rates[n, 1] = 1.0 / (1.0 + k)
        return 0

    unrolled(8, coarsen)

    def make_unit(n, _):
        for m in range(2):
            cu, cv = cs[2 + n, 2 * m + 2], cs[2 + n, 2 * m + 3]
            f, fk = cs[2 + n, 6], cs[2 + n, 7]
            g = cu * cv * cv
            for s in range(2):
                fl = fine_lap(xs[pl.ds(2 * n, 6), 2 * m + s], DIFF[s]) + xp[pl.ds(2 * n + 2, 2), 2 * m + s]
                val = restrict(fl) - coarse_lap(cs[pl.ds(n, 5), 2 * m + s], DIFF[s])[0]
                if s == 0:
                    val = val + f * cu + g
                else:
                    val = val - g + fk * cv
                unit[m, n, s] = val
            unit[m, n, 2] = g
        return 0

    unrolled(4, make_unit)


def coarse_node(src, prm, rates, rate_off, dst, count):
    def step(n, _):
        i = 4 * n
        at = pl.ds(i, 4)
        ra = pl.ds(rate_off + i, 4)
        wu = src[pl.ds(i, 8), 0]
        wv = src[pl.ds(i, 8), 1]
        bu = wu[2:6] + coarse_lap(wu, DIFF[0]) + prm[at, 0]
        bv = wv[2:6] + coarse_lap(wv, DIFF[1]) + prm[at, 1]
        nu, nv = solve(bu, bv, prm[at, 2], rates[ra, 0], rates[ra, 1])
        dst[at, 0] = nu
        dst[at, 1] = nv

    unrolled(count // 4, step)


def two_slices(a, prm, n1, n2, n3, out):
    p1a, p2a, p1b, p2b, rates = prm
    coarse_node(a, p1a, rates, 0, n1, 28)
    coarse_node(n1, p2a, rates, 2, n2, 24)
    coarse_node(n2, p1b, rates, 4, n3, 20)
    coarse_node(n3, p2b, rates, 6, out, 16)


def chain_kernel(a, p1a, p2a, p1b, p2b, rates, out, n1, n2, n3):
    two_slices(a, (p1a, p2a, p1b, p2b, rates), n1, n2, n3, out)


def last_kernel(sc, a, p1a, p2a, p1b, p2b, rates, big, end, prev, res, n1, n2, n3, n4, gs, v1, tp):
    two_slices(a, (p1a, p2a, p1b, p2b, rates), n1, n2, n3, n4)
    core = sc[0]
    yh = sc[1]

    @pl.when(core == 0)
    def _():
        for s in range(2):
            gs[:, s] = a[12:20, s]
            gs[:, 2 + s] = n1[10:18, s]
            gs[:, 4 + s] = n2[8:16, s]

    @pl.when(core != 0)
    def _():
        for s in range(2):
            gs[:, s] = n2[8:16, s]
            gs[:, 2 + s] = n3[6:14, s]
            gs[:, 4 + s] = n4[4:12, s]

    def restrict(x):
        return 0.25 * (x[0, 0] + x[0, 1] + x[1, 0] + x[1, 1])

    def update(i, _):
        row = 2 * yh + i
        at = pl.ds(4 * yh + 2 * i, 2)
        to = pl.ds(2 * i, 2)
        new = []
        for f in range(6):
            x = big[at, f] if f < 4 else end[to, f - 4]
            new.append(x + (gs[row, f] - restrict(x))[None, None])
        u, v = new[0::2], new[1::2]
        bu = prev[to, 0]
        bv = prev[to, 1]
        bu = bu + (gs[row, 0] - restrict(bu))[None, None]
        bv = bv + (gs[row, 1] - restrict(bv))[None, None]
        f, fk = big[at, 6], big[at, 7]
        g = [u[j] * v[j] * v[j] for j in range(3)]
        qu, qv, gq = comb(R1, u), comb(R1, v), comb(R1, g)
        v1[to, 0] = bu + qu + (u[1] - u[0])
        v1[to, 1] = bv + qv + (v[1] - v[0])
        tp[to, 0] = bu + f - f * qu - gq
        tp[to, 1] = bv + gq - fk * qv
        tp[to, 2] = g[1]
        qu, qv, gq = comb(R2, u), comb(R2, v), comb(R2, g)
        tp[to, 3] = qu + (u[2] - u[1])
        tp[to, 4] = qv + (v[2] - v[1])
        tp[to, 5] = f - f * qu - gq
        tp[to, 6] = gq - fk * qv
        tp[to, 7] = g[2]
        tp[to, 8] = bu
        tp[to, 9] = bv
        return 0

    unrolled(6, update)

    def put(node, s, plane, x):
        res[0, node, s, plane, pl.ds(0, 8, stride=2), :] = x[0]
        res[0, node, s, plane, pl.ds(1, 8, stride=2), :] = x[1]

    def node_one(n, _):
        i = 2 + 2 * n
        at = pl.ds(i, 2)
        br = pl.ds(4 * yh + i, 2)
        bu = tp[at, 0] + fine_lap(v1[pl.ds(i - 2, 6), 0], DIFF[0])
        bv = tp[at, 1] + fine_lap(v1[pl.ds(i - 2, 6), 1], DIFF[1])
        nu, nv = solve(bu, bv, tp[at, 2], big[br, 8], big[br, 9])
        tp[at, 3] = tp[at, 3] + nu
        tp[at, 4] = tp[at, 4] + nv
        tp[at, 5] = tp[at, 5] + nu
        tp[at, 6] = tp[at, 6] + nv
        tp[at, 10] = nu
        tp[at, 11] = nv
        return 0

    unrolled(4, node_one)

    for n in range(2):
        i = 4 + 2 * n
        at = pl.ds(i, 2)
        br = pl.ds(4 * yh + i, 2)
        bu = tp[at, 5] + fine_lap(tp[pl.ds(i - 2, 6), 3], DIFF[0])
        bv = tp[at, 6] + fine_lap(tp[pl.ds(i - 2, 6), 4], DIFF[1])
        nu, nv = solve(bu, bv, tp[at, 7], big[br, 8], big[br, 9])
        for d in range(2):
            p = 2 * n + d
            put(2, 0, p, nu[d])
            put(2, 1, p, nv[d])
            for s in range(2):
                put(0, s, p, tp[i + d, 8 + s])
                put(1, s, p, tp[i + d, 10 + s])


def vmem(*shape):
    return pltpu.VMEM(shape, F32)


def shape(*dims):
    return jax.ShapeDtypeStruct(dims, F32)


def program(node_values, start_state, feed_rate, kill_rate):
    t = lax.axis_index("tm")
    core = t % 2
    chip = t // 2
    yh = lax.axis_index("slab") % 2
    left = core == 0
    own = pl.pallas_call(
        pack_kernel, out_shape=shape(4, 10, 2, 8, 128), in_specs=[VM] * 4, out_specs=VM,
        name="pack",
    )(node_values, start_state, feed_rate, kill_rate)
    pair = gather(own, pair_groups()).reshape(8, 10, 2, 8, 128)

    def edge(planes, far):
        w = [far[:, 2 * j:2 * j + 2] for j in range(3)]
        v = first_combo(w, far[:, 6:8])
        return jnp.concatenate([planes.reshape(40, 2, 8, 128), v.reshape(4, 2, 8, 128)])

    lo = lax.ppermute(edge(pair[4:8], pair[2:4]), AX, z_pairs(1))
    hi = lax.ppermute(edge(pair[0:4], pair[4:6]), AX, z_pairs(-1))
    big, unit, start, rates = pl.pallas_call(
        sweep_kernel,
        out_shape=(shape(16, 10, 2, 8, 128), shape(2, 4, 3, 8, 128), shape(8, 2, 8, 128),
                   shape(8, 2, 8, 128)),
        in_specs=[VM] * 3, out_specs=(VM, VM, VM, VM),
        scratch_shapes=[vmem(20, 2, 2, 8, 128), vmem(16, 2, 2, 8, 128), vmem(16, 3, 2, 8, 128),
                        vmem(12, 4, 2, 8, 128), vmem(12, 4, 2, 8, 128), vmem(8, 8, 8, 128)],
        name="sweep", compiler_params=SMALL,
    )(pair, lo, hi)

    def rows(parts):
        return jnp.concatenate([x.reshape(-1, 8, 128) for x in parts])

    both = gather(rows([unit, start]), core_groups())
    units = both[:, :24].reshape(2, 2, 4, 3, 8, 128)
    start = both[0, 24:].reshape(8, 2, 8, 128)
    (p1a, p2a), (p1b, p2b) = units

    def near_planes(x, n):
        return jnp.where(left, x[4 - n:], x[:n])

    def send(parts, step):
        message = rows(parts)
        return lax.ppermute(message, AX, split_pairs(step))

    start4 = jnp.where(left, start[0:4], start[4:8])
    rates4 = jnp.where(left, rates[0:4], rates[4:8])
    near = send([p1a, p2a, p1b, p2b, start4, rates4], 1)
    mid = send([p1a, p2a, p1b, near_planes(p2b, 2), start4, rates4], 2)
    far = send([p1a, near_planes(p2a, 2), start4, jnp.where(left, rates[2:4], rates[4:6])], 3)
    nears = gather(near, core_groups())
    fars = gather(jnp.concatenate([mid, far]), core_groups())

    def pick(part, side, first, planes, fields):
        return part[side, first:first + planes * fields].reshape(planes, fields, 8, 128)

    def window(own, *pieces):
        below = [pick(part, 0, first, planes, own.shape[1]) for part, first, planes in pieces]
        above = [pick(part, 1, first, planes, own.shape[1]) for part, first, planes in pieces]
        return jnp.concatenate(below[::-1] + [own] + above)

    p1a = window(p1a, (nears, 0, 4), (fars, 0, 4), (fars, 58, 4))
    p2a = window(p2a, (nears, 12, 4), (fars, 12, 4), (fars, 70, 2))
    p1b = window(p1b, (nears, 24, 4), (fars, 24, 4))
    p2b = window(p2b, (nears, 36, 4), (fars, 36, 2))
    state = window(start, (nears, 48, 4), (fars, 42, 4), (fars, 76, 4))
    rates = window(rates, (nears, 56, 4), (fars, 50, 4), (fars, 84, 2))
    prm = (p1a, p2a, p1b, p2b, rates)

    lower = yh == 0
    outer = lax.ppermute(jnp.where(lower, big[8:10, 4:6], big[6:8, 4:6]), AX, edge_pairs())
    end = jnp.where(lower, jnp.concatenate([outer, big[2:12, 4:6]]),
                    jnp.concatenate([big[4:14, 4:6], outer]))
    prev = lax.ppermute(end, AX, slice_pairs())
    prev = jnp.where(t == 0, jnp.where(lower, big[0:12, 0:2], big[4:16, 0:2]), prev)

    scratch = [vmem(28, 2, 8, 128), vmem(24, 2, 8, 128), vmem(20, 2, 8, 128)]

    for turn in range(7):
        out = pl.pallas_call(
            chain_kernel, out_shape=shape(16, 2, 8, 128), in_specs=[VM] * 6, out_specs=VM,
            scratch_shapes=scratch, name="chain", compiler_params=SMALL,
        )(state, *prm)
        first = lax.ppermute(out[:8], AX, turn_pairs(turn))
        rest = lax.ppermute(out[8:], AX, turn_pairs(turn))
        moved = jnp.concatenate([first, rest])
        moved = gather(moved, core_groups()).reshape(32, 2, 8, 128)
        state = jnp.where(chip == turn + 1, moved, state)

    scalars = jnp.stack([core, yh]).astype(jnp.int32)
    return pl.pallas_call(
        last_kernel, out_shape=shape(1, 3, 2, 4, 16, 128), in_specs=[SM] + [VM] * 9, out_specs=VM,
        scratch_shapes=scratch + [
            vmem(16, 2, 8, 128), vmem(8, 6, 8, 128), vmem(12, 2, 2, 8, 128), vmem(12, 12, 2, 8, 128)],
        name="last", compiler_params=SMALL,
    )(scalars, state, *prm, big, end, prev)


def solution(mesh):
    return jax.shard_map(
        program,
        mesh=mesh,
        in_specs=(
            P("tm", None, None, "slab", None, None),
            P("tm", None, "slab", None, None),
            P("slab", None, None),
            P("slab", None, None),
        ),
        out_specs=P("tm", None, None, "slab", None, None),
        check_vma=False,
    )
```

```python
import jax
import jax.numpy as jnp
from jax import lax
from jax.experimental import pallas as pl
from jax.experimental.pallas import tpu as pltpu
from jax.sharding import PartitionSpec as P


AX = ("tm", "slab")
F32 = jnp.float32
W1 = (5.0 / 12.0, 2.0 / 3.0, -1.0 / 12.0)
W2 = (-1.0 / 12.0, 2.0 / 3.0, 5.0 / 12.0)
R1 = (5.0 / 12.0, 2.0 / 3.0 - 1.0, -1.0 / 12.0)
R2 = (-1.0 / 12.0, 2.0 / 3.0, 5.0 / 12.0 - 1.0)
DIFF = (0.1, 0.05)
VM = pl.BlockSpec(memory_space=pltpu.VMEM)
SM = pl.BlockSpec(memory_space=pltpu.SMEM)
SMALL = pltpu.CompilerParams(vmem_limit_bytes=16 * 1024 * 1024)


def flat(z, yh, chip, core):
    return (2 * chip + core) * 32 + (z % 16) * 2 + yh


def everyone():
    return [(z, yh, chip, core) for z in range(16) for yh in range(2)
            for chip in range(8) for core in range(2)]


def pair_groups():
    return [[flat(z, 0, c, k), flat(z, 1, c, k)] for z in range(16) for c in range(8) for k in range(2)]


def core_groups():
    return [[flat(z, h, c, 0), flat(z, h, c, 1)] for z in range(16) for h in range(2) for c in range(8)]


def z_pairs(step):
    return [(flat(z, h, c, k), flat(z + step, h, c, k)) for z, h, c, k in everyone()]


def split_pairs(step):
    return [(flat(z, h, c, k), flat(z + (step if k == 0 else -step), h, c, k))
            for z, h, c, k in everyone()]


def slice_pairs():
    return [(t * 32 + s, (t + 1) * 32 + s) for t in range(15) for s in range(32)]


def turn_pairs(turn):
    return [(flat(z, h, turn, k), flat(z + (2 if k == 0 else -2), h ^ k, turn + 1, k))
            for z in range(16) for h in range(2) for k in range(2)]


def gather(x, groups):
    return lax.all_gather(x, AX, axis=0, axis_index_groups=groups, tiled=False)


def lane(x, n):
    return pltpu.roll(x, n % 128, x.ndim - 1)


def sub(x, n):
    return pltpu.roll(x, n % 8, x.ndim - 2)


def fine_lap(win, coef):
    n = win.shape[0] - 4
    mid = win[2:n + 2]
    near = win[1:n + 1] + win[3:n + 3]
    far = win[0:n] + win[4:n + 4]
    even = mid[:, 0]
    odd = mid[:, 1]
    even_up, even_dn = sub(even, 1), sub(even, -1)
    odd_up, odd_dn = sub(odd, 1), sub(odd, -1)
    nx = jnp.stack([odd + odd_up, even + even_dn], axis=1)
    fx = jnp.stack([even_up + even_dn, odd_up + odd_dn], axis=1)
    near = near + nx + (lane(mid, 1) + lane(mid, -1))
    far = far + fx + (lane(mid, 2) + lane(mid, -2))
    return (coef * 16.0 / 12.0) * near - (coef / 12.0) * far - (coef * 90.0 / 12.0) * mid


def coarse_lap(win, coef):
    n = win.shape[0] - 4
    mid = win[2:n + 2]
    near = win[1:n + 1] + win[3:n + 3] + (sub(mid, 1) + sub(mid, -1))
    far = win[0:n] + win[4:n + 4] + (sub(mid, 2) + sub(mid, -2))
    near_y = lane(mid, 1) + lane(mid, -1)
    far_y = lane(mid, 2) + lane(mid, -2)
    c = coef / 12.0
    return (4.0 * c) * near - (0.25 * c) * far + (16.0 * c) * near_y - c * far_y - (45.0 * c) * mid


def solve(bu, bv, g, ru, rv):
    u = (bu - g) * ru
    v = (bv + g) * rv
    g = u * v * v
    return (bu - g) * ru, (bv + g) * rv


def comb(w, xs):
    return w[0] * xs[0] + w[1] * xs[1] + w[2] * xs[2]


def unrolled(count, step):
    for n in range(count):
        step(n, 0)


def pack_kernel(nv, st, fr, kr, out):
    for p in range(4):
        for par in range(2):
            rows = pl.ds(par, 8, stride=2)
            for j in range(3):
                for s in range(2):
                    out[p, 2 * j + s, par] = nv[0, j, s, p, rows, :]
            for s in range(2):
                out[p, 6 + s, par] = st[0, s, p, rows, :]
            out[p, 8, par] = fr[p, rows, :]
            out[p, 9, par] = kr[p, rows, :]


def first_combo(w, start):
    return start + (5.0 / 12.0 - 1.0) * w[0] + (2.0 / 3.0) * w[1] - (1.0 / 12.0) * w[2]


def sweep_kernel(pair, lo, hi, big, unit, start, rates, v1, v2, b2, xs, xp, cs):
    segs = ((lo, 2, 4), (pair, 6, 8), (hi, 14, 4))

    def raw(ref, i, f):
        if ref is pair:
            return ref[pl.ds(i, 2), f]
        return jnp.stack([ref[i * 10 + f], ref[i * 10 + 10 + f]])

    for s in range(2):
        v1[0, s] = lo[40 + s]
        v1[1, s] = lo[42 + s]
        v1[18, s] = hi[40 + s]
        v1[19, s] = hi[42 + s]

    for ref, base, count in segs:
        def load_v1(n, _, ref=ref, base=base):
            i = 2 * n
            for s in range(2):
                w = [raw(ref, i, 2 * j + s) for j in range(3)]
                start = raw(ref, i, 6 + s)
                v1[pl.ds(base + i, 2), s] = first_combo(w, start)
            return 0

        unrolled(count // 2, load_v1)

    for ref, base, count in segs:
        def node_one(n, _, ref=ref, base=base):
            i = 2 * n
            p = base + i
            q = p - 2
            u = [raw(ref, i, 2 * j) for j in range(3)]
            v = [raw(ref, i, 2 * j + 1) for j in range(3)]
            su, sv = raw(ref, i, 6), raw(ref, i, 7)
            f = raw(ref, i, 8)
            fk = f + raw(ref, i, 9)
            ru = 1.0 / (1.0 + f)
            rv = 1.0 / (1.0 + fk)
            g = [u[j] * v[j] * v[j] for j in range(3)]
            gq = comb(R1, g)
            bu = su + f - f * comb(R1, u) - gq + fine_lap(v1[pl.ds(p - 2, 6), 0], DIFF[0])
            bv = sv + gq - fk * comb(R1, v) + fine_lap(v1[pl.ds(p - 2, 6), 1], DIFF[1])
            nu, nv = solve(bu, bv, g[1], ru, rv)
            at = pl.ds(q, 2)
            big[at, 0] = su
            big[at, 1] = sv
            big[at, 2] = nu
            big[at, 3] = nv
            big[at, 6] = f
            big[at, 7] = fk
            big[at, 8] = ru
            big[at, 9] = rv
            qu, qv = comb(R2, u), comb(R2, v)
            gq = comb(R2, g)
            v2[at, 0] = nu + qu + (u[2] - u[1])
            v2[at, 1] = nv + qv + (v[2] - v[1])
            b2[at, 0] = nu + f - f * qu - gq
            b2[at, 1] = nv + gq - fk * qv
            b2[at, 2] = g[2]
            return 0

        unrolled(count // 2, node_one)

    def node_two(n, _):
        q = 2 + 2 * n
        at = pl.ds(q, 2)
        bu = b2[at, 0] + fine_lap(v2[pl.ds(q - 2, 6), 0], DIFF[0])
        bv = b2[at, 1] + fine_lap(v2[pl.ds(q - 2, 6), 1], DIFF[1])
        nu, nv = solve(bu, bv, b2[at, 2], big[at, 8], big[at, 9])
        big[at, 4] = nu
        big[at, 5] = nv
        return 0

    unrolled(6, node_two)

    def integrals(n, _):
        q = 2 + 2 * n
        at = pl.ds(q, 2)
        u = [big[at, 2 * j] for j in range(3)]
        v = [big[at, 2 * j + 1] for j in range(3)]
        f, fk = big[at, 6], big[at, 7]
        g = [u[j] * v[j] * v[j] for j in range(3)]
        to = pl.ds(2 * n, 2)
        for m, w in enumerate((W1, W2)):
            xu, xv, gx = comb(w, u), comb(w, v), comb(w, g)
            xs[to, 2 * m] = xu
            xs[to, 2 * m + 1] = xv
            xp[to, 2 * m] = f - f * xu - gx
            xp[to, 2 * m + 1] = gx - fk * xv
        return 0

    unrolled(6, integrals)

    def restrict(x):
        return 0.25 * (x[0, 0] + x[0, 1] + x[1, 0] + x[1, 1])

    def coarsen(n, _):
        at = pl.ds(2 * n, 2)
        for f in range(6 if 1 <= n <= 6 else 4):
            cs[n, f] = restrict(big[at, f])
        f = restrict(big[at, 6])
        k = restrict(big[at, 7])
        cs[n, 6] = f
        cs[n, 7] = k
        start[n, 0] = cs[n, 0]
        start[n, 1] = cs[n, 1]
        rates[n, 0] = 1.0 / (1.0 + f)
        rates[n, 1] = 1.0 / (1.0 + k)
        return 0

    unrolled(8, coarsen)

    def make_unit(n, _):
        for m in range(2):
            cu, cv = cs[2 + n, 2 * m + 2], cs[2 + n, 2 * m + 3]
            f, fk = cs[2 + n, 6], cs[2 + n, 7]
            g = cu * cv * cv
            for s in range(2):
                fl = fine_lap(xs[pl.ds(2 * n, 6), 2 * m + s], DIFF[s]) + xp[pl.ds(2 * n + 2, 2), 2 * m + s]
                val = restrict(fl) - coarse_lap(cs[pl.ds(n, 5), 2 * m + s], DIFF[s])[0]
                if s == 0:
                    val = val + f * cu + g
                else:
                    val = val - g + fk * cv
                unit[m, n, s] = val
            unit[m, n, 2] = g
        return 0

    unrolled(4, make_unit)


def coarse_node(src, prm, rates, rate_off, dst, count):
    def step(n, _):
        i = 4 * n
        at = pl.ds(i, 4)
        ra = pl.ds(rate_off + i, 4)
        wu = src[pl.ds(i, 8), 0]
        wv = src[pl.ds(i, 8), 1]
        bu = wu[2:6] + coarse_lap(wu, DIFF[0]) + prm[at, 0]
        bv = wv[2:6] + coarse_lap(wv, DIFF[1]) + prm[at, 1]
        nu, nv = solve(bu, bv, prm[at, 2], rates[ra, 0], rates[ra, 1])
        dst[at, 0] = nu
        dst[at, 1] = nv

    unrolled(count // 4, step)


def two_slices(a, prm, n1, n2, n3, out):
    p1a, p2a, p1b, p2b, rates = prm
    coarse_node(a, p1a, rates, 0, n1, 28)
    coarse_node(n1, p2a, rates, 2, n2, 24)
    coarse_node(n2, p1b, rates, 4, n3, 20)
    coarse_node(n3, p2b, rates, 6, out, 16)


def chain_kernel(a, p1a, p2a, p1b, p2b, rates, out, n1, n2, n3):
    two_slices(a, (p1a, p2a, p1b, p2b, rates), n1, n2, n3, out)


def last_kernel(sc, a, p1a, p2a, p1b, p2b, rates, big, end, prev, res, n1, n2, n3, n4, gs, v1, tp):
    two_slices(a, (p1a, p2a, p1b, p2b, rates), n1, n2, n3, n4)
    core = sc[0]
    yh = sc[1]

    @pl.when(core == 0)
    def _():
        for s in range(2):
            gs[:, s] = a[12:20, s]
            gs[:, 2 + s] = n1[10:18, s]
            gs[:, 4 + s] = n2[8:16, s]

    @pl.when(core != 0)
    def _():
        for s in range(2):
            gs[:, s] = n2[8:16, s]
            gs[:, 2 + s] = n3[6:14, s]
            gs[:, 4 + s] = n4[4:12, s]

    def restrict(x):
        return 0.25 * (x[0, 0] + x[0, 1] + x[1, 0] + x[1, 1])

    def update(i, _):
        row = 2 * yh + i
        at = pl.ds(4 * yh + 2 * i, 2)
        to = pl.ds(2 * i, 2)
        new = []
        for f in range(6):
            x = big[at, f] if f < 4 else end[to, f - 4]
            new.append(x + (gs[row, f] - restrict(x))[None, None])
        u, v = new[0::2], new[1::2]
        bu = prev[to, 0]
        bv = prev[to, 1]
        bu = bu + (gs[row, 0] - restrict(bu))[None, None]
        bv = bv + (gs[row, 1] - restrict(bv))[None, None]
        f, fk = big[at, 6], big[at, 7]
        g = [u[j] * v[j] * v[j] for j in range(3)]
        qu, qv, gq = comb(R1, u), comb(R1, v), comb(R1, g)
        v1[to, 0] = bu + qu + (u[1] - u[0])
        v1[to, 1] = bv + qv + (v[1] - v[0])
        tp[to, 0] = bu + f - f * qu - gq
        tp[to, 1] = bv + gq - fk * qv
        tp[to, 2] = g[1]
        qu, qv, gq = comb(R2, u), comb(R2, v), comb(R2, g)
        tp[to, 3] = qu + (u[2] - u[1])
        tp[to, 4] = qv + (v[2] - v[1])
        tp[to, 5] = f - f * qu - gq
        tp[to, 6] = gq - fk * qv
        tp[to, 7] = g[2]
        tp[to, 8] = bu
        tp[to, 9] = bv
        return 0

    unrolled(6, update)

    def put(node, s, plane, x):
        res[0, node, s, plane, pl.ds(0, 8, stride=2), :] = x[0]
        res[0, node, s, plane, pl.ds(1, 8, stride=2), :] = x[1]

    def node_one(n, _):
        i = 2 + 2 * n
        at = pl.ds(i, 2)
        br = pl.ds(4 * yh + i, 2)
        bu = tp[at, 0] + fine_lap(v1[pl.ds(i - 2, 6), 0], DIFF[0])
        bv = tp[at, 1] + fine_lap(v1[pl.ds(i - 2, 6), 1], DIFF[1])
        nu, nv = solve(bu, bv, tp[at, 2], big[br, 8], big[br, 9])
        tp[at, 3] = tp[at, 3] + nu
        tp[at, 4] = tp[at, 4] + nv
        tp[at, 5] = tp[at, 5] + nu
        tp[at, 6] = tp[at, 6] + nv
        tp[at, 10] = nu
        tp[at, 11] = nv
        return 0

    unrolled(4, node_one)

    for n in range(2):
        i = 4 + 2 * n
        at = pl.ds(i, 2)
        br = pl.ds(4 * yh + i, 2)
        bu = tp[at, 5] + fine_lap(tp[pl.ds(i - 2, 6), 3], DIFF[0])
        bv = tp[at, 6] + fine_lap(tp[pl.ds(i - 2, 6), 4], DIFF[1])
        nu, nv = solve(bu, bv, tp[at, 7], big[br, 8], big[br, 9])
        for d in range(2):
            p = 2 * n + d
            put(2, 0, p, nu[d])
            put(2, 1, p, nv[d])
            for s in range(2):
                put(0, s, p, tp[i + d, 8 + s])
                put(1, s, p, tp[i + d, 10 + s])


def vmem(*shape):
    return pltpu.VMEM(shape, F32)


def shape(*dims):
    return jax.ShapeDtypeStruct(dims, F32)


def program(node_values, start_state, feed_rate, kill_rate):
    t = lax.axis_index("tm")
    core = t % 2
    chip = t // 2
    yh = lax.axis_index("slab") % 2
    left = core == 0
    own = pl.pallas_call(
        pack_kernel, out_shape=shape(4, 10, 2, 8, 128), in_specs=[VM] * 4, out_specs=VM,
        name="pack",
    )(node_values, start_state, feed_rate, kill_rate)
    pair = gather(own, pair_groups()).reshape(8, 10, 2, 8, 128)

    def edge(planes, far):
        w = [far[:, 2 * j:2 * j + 2] for j in range(3)]
        v = first_combo(w, far[:, 6:8])
        return jnp.concatenate([planes.reshape(40, 2, 8, 128), v.reshape(4, 2, 8, 128)])

    lo = lax.ppermute(edge(pair[4:8], pair[2:4]), AX, z_pairs(1))
    hi = lax.ppermute(edge(pair[0:4], pair[4:6]), AX, z_pairs(-1))
    big, unit, start, rates = pl.pallas_call(
        sweep_kernel,
        out_shape=(shape(16, 10, 2, 8, 128), shape(2, 4, 3, 8, 128), shape(8, 2, 8, 128),
                   shape(8, 2, 8, 128)),
        in_specs=[VM] * 3, out_specs=(VM, VM, VM, VM),
        scratch_shapes=[vmem(20, 2, 2, 8, 128), vmem(16, 2, 2, 8, 128), vmem(16, 3, 2, 8, 128),
                        vmem(12, 4, 2, 8, 128), vmem(12, 4, 2, 8, 128), vmem(8, 8, 8, 128)],
        name="sweep", compiler_params=SMALL,
    )(pair, lo, hi)

    def rows(parts):
        return jnp.concatenate([x.reshape(-1, 8, 128) for x in parts])

    lower = yh == 0
    outer = jnp.where(lower, big[8:10, 4:6], big[6:8, 4:6])
    both = gather(rows([unit, start, outer]), core_groups())
    outer = both[:, 40:]
    units = both[:, :24].reshape(2, 2, 4, 3, 8, 128)
    start = both[0, 24:40].reshape(8, 2, 8, 128)
    (p1a, p2a), (p1b, p2b) = units

    def near_planes(x, n):
        return jnp.where(left, x[4 - n:], x[:n])

    def send(parts, step):
        message = rows(parts)
        return lax.ppermute(message, AX, split_pairs(step))

    start4 = jnp.where(left, start[0:4], start[4:8])
    rates4 = jnp.where(left, rates[0:4], rates[4:8])
    near = send([p1a, p2a, p1b, p2b, start4, rates4, outer], 1)
    mid = send([p1a, p2a, p1b, near_planes(p2b, 2), start4, rates4], 2)
    far = send([p1a, near_planes(p2a, 2), start4, jnp.where(left, rates[2:4], rates[4:6])], 3)
    nears = gather(near, core_groups())
    far_rows = jnp.concatenate([mid, far])
    fars = gather(far_rows, core_groups())

    def pick(part, side, first, planes, fields):
        return part[side, first:first + planes * fields].reshape(planes, fields, 8, 128)

    def window(own, *pieces):
        below = [pick(part, 0, first, planes, own.shape[1]) for part, first, planes in pieces]
        above = [pick(part, 1, first, planes, own.shape[1]) for part, first, planes in pieces]
        return jnp.concatenate(below[::-1] + [own] + above)

    p1a = window(p1a, (nears, 0, 4), (fars, 0, 4), (fars, 58, 4))
    p2a = window(p2a, (nears, 12, 4), (fars, 12, 4), (fars, 70, 2))
    p1b = window(p1b, (nears, 24, 4), (fars, 24, 4))
    p2b = window(p2b, (nears, 36, 4), (fars, 36, 2))
    state = window(start, (nears, 48, 4), (fars, 42, 4), (fars, 76, 4))
    rates = window(rates, (nears, 56, 4), (fars, 50, 4), (fars, 84, 2))
    prm = (p1a, p2a, p1b, p2b, rates)

    outer = jnp.where(lower, nears[0, 64:], nears[1, 64:])
    outer = jnp.where(left, outer[:8], outer[8:]).reshape(2, 2, 2, 8, 128)
    end = jnp.where(lower, jnp.concatenate([outer, big[2:12, 4:6]]),
                    jnp.concatenate([big[4:14, 4:6], outer]))
    prev = lax.ppermute(end, AX, slice_pairs())
    prev = jnp.where(t == 0, jnp.where(lower, big[0:12, 0:2], big[4:16, 0:2]), prev)

    scratch = [vmem(28, 2, 8, 128), vmem(24, 2, 8, 128), vmem(20, 2, 8, 128)]

    for turn in range(7):
        out = pl.pallas_call(
            chain_kernel, out_shape=shape(16, 2, 8, 128), in_specs=[VM] * 6, out_specs=VM,
            scratch_shapes=scratch, name="chain", compiler_params=SMALL,
        )(state, *prm)
        moved = lax.ppermute(out, AX, turn_pairs(turn))
        moved = gather(moved, core_groups()).reshape(32, 2, 8, 128)
        state = jnp.where(chip == turn + 1, moved, state)

    scalars = jnp.stack([core, yh]).astype(jnp.int32)
    return pl.pallas_call(
        last_kernel, out_shape=shape(1, 3, 2, 4, 16, 128), in_specs=[SM] + [VM] * 9, out_specs=VM,
        scratch_shapes=scratch + [
            vmem(16, 2, 8, 128), vmem(8, 6, 8, 128), vmem(12, 2, 2, 8, 128), vmem(12, 12, 2, 8, 128)],
        name="last", compiler_params=SMALL,
    )(scalars, state, *prm, big, end, prev)


def solution(mesh):
    return jax.shard_map(
        program,
        mesh=mesh,
        in_specs=(
            P("tm", None, None, "slab", None, None),
            P("tm", None, "slab", None, None),
            P("slab", None, None),
            P("slab", None, None),
        ),
        out_specs=P("tm", None, None, "slab", None, None),
        check_vma=False,
    )
```
